32 devices in a mesh: grp: 4 (over z), fsdp: 8 (over y, x, core).
Axes of the slice: x: 2, y: 2, z: 4, core: 2. Of those that a mesh axis runs over, the one named last changes fastest.
Arguments:
- acts: bfloat16 [64, 128, 4096], P(('grp', 'fsdp'))
- out_grads: bfloat16 [64, 128, 1024], P(('grp', 'fsdp'))
- doc_lengths: int32 [64], P(('grp', 'fsdp')), may hold values from 32 to 128
- proj_in: bfloat16 [64, 4096], replicated, may hold values from -0.09375 to 0.09375
- proj_out: bfloat16 [64, 1024], replicated, may hold values from -0.1875 to 0.1875
- store_grads: bfloat16 [7168, 4096], P(('grp', 'fsdp')), may hold values from -6 to 6
- queries: bfloat16 [512, 4096], P('fsdp'), may hold values from -6 to 6
Outputs:
- new_grads: bfloat16 [64, 4096], P(('grp', 'fsdp'))
- store_scores: bfloat16 [7168, 512], P(('grp', 'fsdp'))
- new_scores: bfloat16 [64, 512], P(('grp', 'fsdp'))
The draws below stay inside these ranges and needn't reach their ends.
All inputs are finite; a program needn't handle non-finite values.
Results may differ from the reference program's by a relative error of at most 0.012.
The reference program's roundings to bfloat16 on the way (of `prepared`) count: a program that leaves them out, or rounds other values in their place, can miss the bound.
Values may be sent and summed in bfloat16 or wider, within the bound.
A program may use at most 64 MiB of HBM per device.

```python
import jax
import jax.numpy as jnp
from jax import lax

D = 4096
KV = 1024
R = 64
LEN = 128
QUERIES = 512
DOCS = 64
STORE = 7168


def document_scales(key):
    doc_index = jnp.arange(DOCS).astype(jnp.float32)
    rising = 1.0 + 2.0 * doc_index / max(DOCS - 1, 1)
    spread = jnp.exp(jax.random.uniform(key, (DOCS,), jnp.float32, -1.15, 1.15))
    return rising * spread


def token_field(key, features):
    keys = jax.random.split(key, 3)
    scales = document_scales(keys[0])
    noise = jax.random.normal(keys[1], (DOCS, LEN, features), jnp.float32)
    center = 0.7 * jax.random.normal(keys[2], (features,), jnp.float32)
    return scales[:, None, None] * (noise + center)


def draw_acts(key, part):
    return token_field(jax.random.fold_in(key, 101), D).astype(jnp.bfloat16)


def draw_out_grads(key, part):
    return token_field(jax.random.fold_in(key, 202), KV).astype(jnp.bfloat16)


def touch_ends(entries, stream_key, least, high):
    longest = entries.shape.index(max(entries.shape))
    spots = []
    for shift in (0, 1):
        where = [jax.random.randint(jax.random.fold_in(stream_key, axis), (), 0, length) for axis, length in enumerate(entries.shape)]
        where[longest] = (where[longest] + shift) % entries.shape[longest]
        spots.append(tuple(where))
    return entries.at[spots[0]].set(least).at[spots[1]].set(high)


def steps_of(stream_key, shape, cuts, low, high):
    loudness = 1.0
    for position, blocks in cuts:
        heights = jax.random.uniform(jax.random.fold_in(jax.random.fold_in(stream_key, 6), position), (blocks,), jnp.float32, low / len(cuts), high / len(cuts))
        loudness = loudness * jnp.repeat(jnp.exp(heights), shape[position] // blocks).reshape((-1,) + (1,) * (len(shape) - 1 - position))
    return loudness


def centred(rng, dims, width, limit, pieces=(), kind=jnp.bfloat16):
    array = jax.random.normal(rng, dims, jnp.float32) * width
    if len(pieces) > 0:
        array = steps_of(rng, dims, pieces, -0.22, 0.18) * array
    return jnp.clip(array, min=-limit, max=limit).astype(kind)


def setup_inputs(seed: int = 0) -> dict:
    splits = jax.random.split(jax.random.key(seed), 8)
    return {
        "acts": draw_acts(jax.random.fold_in(splits[7], 71), 0),
        "out_grads": draw_out_grads(jax.random.fold_in(splits[7], 71), 0),
        "doc_lengths": touch_ends(jax.random.randint(splits[2], (DOCS,), LEN // 4, LEN + 1), jax.random.fold_in(splits[2], 1), LEN // 4, LEN).astype(jnp.int32),
        "proj_in": centred(splits[3], (R, D), D ** -0.5, 0.09375),
        "proj_out": centred(splits[4], (R, KV), KV ** -0.5, 0.1875),
        "store_grads": centred(splits[5], (STORE, R * R), 1.0, 6.0, ((0, 32),)),
        "queries": centred(splits[6], (QUERIES, R * R), 1.0, 6.0, ((0, 8),)),
    }


def damped_inverse(summed, token_count, identity_matrix):
    covariance = summed / token_count
    damped = covariance + 0.1 * jnp.trace(covariance) / R * identity_matrix
    lower_factor = jnp.linalg.cholesky(damped)
    return jax.scipy.linalg.cho_solve((lower_factor, True), identity_matrix)

def precondition(query_rows, out_inverse, in_inverse):
    query_mats = query_rows.astype(jnp.float32).reshape(query_rows.shape[0], R, R)
    half_done = jnp.einsum('ab,qbc->qac', out_inverse, query_mats, precision=lax.Precision.HIGHEST)
    precond = jnp.einsum('qac,cd->qad', half_done, in_inverse, precision=lax.Precision.HIGHEST)
    return precond.reshape(query_rows.shape[0], R * R).astype(jnp.bfloat16)

def reference(acts, out_grads, doc_lengths, proj_in, proj_out, store_grads, queries):
    positions = lax.broadcasted_iota(jnp.int32, (DOCS, LEN), 1)
    valid_mask = (positions < doc_lengths[:, None]).astype(jnp.float32)
    in_proj = jnp.dot(acts.reshape(DOCS * LEN, D).astype(jnp.float32), proj_in.T.astype(jnp.float32), preferred_element_type=jnp.float32).reshape(DOCS, LEN, R)
    out_proj = jnp.dot(out_grads.reshape(DOCS * LEN, KV).astype(jnp.float32), proj_out.T.astype(jnp.float32), preferred_element_type=jnp.float32).reshape(DOCS, LEN, R)
    in_masked = in_proj * valid_mask[:, :, None]
    out_masked = out_proj * valid_mask[:, :, None]
    in_factor = jnp.einsum('dta,dtb->ab', in_masked, in_proj, precision=lax.Precision.HIGHEST)
    out_factor = jnp.einsum('dta,dtb->ab', out_masked, out_proj, precision=lax.Precision.HIGHEST)
    token_count = jnp.sum(valid_mask)
    per_doc = jnp.einsum('dta,dtb->dab', out_masked, in_proj, precision=lax.Precision.HIGHEST)
    per_doc = per_doc / doc_lengths.astype(jnp.float32)[:, None, None]
    new_grads = per_doc.reshape(DOCS, R * R).astype(jnp.bfloat16)
    identity_matrix = jnp.eye(R, dtype=jnp.float32)
    in_inverse = damped_inverse(in_factor, token_count, identity_matrix)
    out_inverse = damped_inverse(out_factor, token_count, identity_matrix)
    prepared = precondition(queries, out_inverse, in_inverse)
    store_scores = jnp.dot(store_grads.astype(jnp.float32), prepared.T.astype(jnp.float32), preferred_element_type=jnp.float32).astype(jnp.bfloat16)
    new_scores = jnp.dot(new_grads.astype(jnp.float32), prepared.T.astype(jnp.float32), preferred_element_type=jnp.float32).astype(jnp.bfloat16)
    return (new_grads, store_scores, new_scores)
```

```python
import functools

import jax
import jax.numpy as jnp
from jax import lax
from jax.experimental import pallas as pl
from jax.experimental.pallas import tpu as pltpu
from jax.sharding import PartitionSpec as P

F32 = jnp.float32
BF16 = jnp.bfloat16
ANY = pl.ANY
VMEM = pltpu.VMEM
HIGHEST = lax.Precision.HIGHEST
NT = (((1,), (1,)), ((), ()))
TN = (((0,), (0,)), ((), ()))


def invert_pair(matrix, rank):
    lanes = lax.broadcasted_iota(jnp.int32, (8, 2 * rank), 1)
    subs = lax.broadcasted_iota(jnp.int32, (8, 2 * rank), 0)
    left = lanes < rank
    local = jnp.where(left, lanes, lanes - rank)
    blocks = [matrix[i : i + 8, :] for i in range(0, rank, 8)]
    for first in range(0, rank, AHEAD):
        ahead = range(first, first + AHEAD)
        columns = [
            [jnp.take_along_axis(block, jnp.where(left, k, rank + k), axis=1) for block in blocks]
            for k in ahead
        ]
        for k in ahead:
            at, row = k // 8, k % 8
            column = columns[k - first]
            inverse_pivot = 1.0 / column[at][row : row + 1, :]
            at_pivot = local == k
            scaled = jnp.where(at_pivot[:1], 1.0, blocks[at][row : row + 1, :]) * inverse_pivot
            for later in range(k + 1 - first, AHEAD):
                part = columns[later][at][row : row + 1, :] * inverse_pivot
                reduced = [c - d * part for c, d in zip(columns[later], column)]
                reduced[at] = jnp.where(subs == row, part, reduced[at])
                columns[later] = reduced
            reduced = [jnp.where(at_pivot, 0.0, c) - d * scaled for c, d in zip(blocks, column)]
            reduced[at] = jnp.where(subs == row, scaled, reduced[at])
            blocks = reduced
    return jnp.concatenate(blocks, axis=0)


def split3(value):
    high = value.astype(BF16)
    rest = value - high.astype(F32)
    middle = rest.astype(BF16)
    low = (rest - middle.astype(F32)).astype(BF16)
    return high, middle, low


def send_order(n_chips, unit_chips, cut):
    slots = [(e, i) for e in range(n_chips // unit_chips) for i in range(unit_chips)][1:]
    straight = [s for s in slots if s[0] == 0 or s[1] == 0]
    turning = [s for s in slots if s[0] != 0 and s[1] != 0]
    return [(s, p) for p in range(cut) for s in straight] + [(s, p) for p in range(cut) for s in turning]


def influence_kernel(
    n_grp, n_fsdp,
    lengths, acts, out_grads, proj_in, proj_out, queries, store,
    new_grads, store_out, new_out,
    acts_v, outg_v, pin_v, pout_v, raw, turned, own, other, score_rows, work, order_m,
    pieces, plane_slots, column_slots, totals,
    load_sems, gs, gr, fs, fr, ps, pr, cs, cr, ts, tr,
):
    g = lax.axis_index("grp")
    f = lax.axis_index("fsdp")
    n_docs, length, features = acts.shape
    rank = proj_in.shape[0]
    here, width = queries.shape
    stored = store.shape[0]
    n_chips = n_fsdp // 2
    chip = f // 2
    core = lax.rem(f, 2)
    cut = here // PIECE
    share = rank // n_fsdp
    pitch = rank + 8
    mine = n_chips * here
    unit_chips = UNIT // here
    n_units = n_chips // unit_chips
    my_unit = chip // unit_chips
    my_place = lax.rem(chip, unit_chips)
    mesh_id = pl.DeviceIdType.MESH

    def in_plane(d):
        return {"grp": g, "fsdp": lax.rem(f + d, n_fsdp)}

    def in_column(d):
        return {"grp": lax.rem(g + d, n_grp), "fsdp": f}

    def rows_of(index, p):
        return raw.at[pl.ds(pl.multiple_of(index * here + p * PIECE, PIECE), PIECE)]

    def shard_copy(slot, p):
        e, i = slot
        target = lax.rem(my_unit + e, n_units) * unit_chips + lax.rem(my_place + i, unit_chips)
        at = (e * unit_chips + i) * cut + p
        return pltpu.make_async_remote_copy(
            src_ref=queries.at[pl.ds(p * PIECE, PIECE)], dst_ref=rows_of(chip, p),
            send_sem=gs.at[at], recv_sem=gr.at[at],
            device_id={"grp": g, "fsdp": target * 2 + core}, device_id_type=mesh_id)

    def pass_copy(k):
        rows = pl.ds(k * (width // PASSES), width // PASSES)
        return pltpu.make_async_remote_copy(
            src_ref=own.at[rows], dst_ref=other.at[rows],
            send_sem=fs.at[k], recv_sem=fr.at[k],
            device_id={"grp": g, "fsdp": f + 1 - 2 * core}, device_id_type=mesh_id)

    own_rows = raw.at[pl.ds(pl.multiple_of(chip * here, here), here)]
    loads = [
        pltpu.make_async_copy(src, dst, load_sems.at[i])
        for i, (src, dst) in enumerate((
            (acts, acts_v), (proj_in, pin_v), (out_grads, outg_v), (proj_out, pout_v),
            (queries, own_rows), (store, score_rows.at[pl.ds(0, stored)])))
    ]
    for load in loads:
        load.start()

    barrier = pltpu.get_barrier_semaphore()

    def greet_plane(d, _):
        pl.semaphore_signal(barrier, inc=1, device_id=in_plane(d), device_id_type=mesh_id)
        return 0

    def greet_column(d, _):
        pl.semaphore_signal(barrier, inc=1, device_id=in_column(d), device_id_type=mesh_id)
        return 0

    lax.fori_loop(1, n_fsdp, greet_plane, 0)
    lax.fori_loop(1, n_grp, greet_column, 0)

    wide_row = lax.broadcasted_iota(jnp.int32, order_m.shape, 0)
    wide_lane = lax.broadcasted_iota(jnp.int32, order_m.shape, 1)
    from_core = lax.rem(wide_lane // here, 2)
    from_row = jnp.where(from_core == core, 0, mine) + wide_lane // (2 * here) * here + lax.rem(wide_lane, here)
    order_m[...] = jnp.where(wide_row == from_row, 1.0, 0.0).astype(BF16)

    order = send_order(n_chips, unit_chips, cut)
    marks = [0] + [len(order) * m // 12 for m in MARKS] + [len(order)]

    def send_part(j):
        for slot, p in order[marks[j] : marks[j + 1]]:
            shard_copy(slot, p).start()

    pl.semaphore_wait(barrier, n_fsdp - 1 + n_grp - 1)
    send_part(0)
    for load in loads[:4]:
        load.wait()

    tokens = lax.broadcasted_iota(jnp.int32, (length, 2 * rank), 0)
    lanes = lax.broadcasted_iota(jnp.int32, (rank, 2 * rank), 1)
    rows = lax.broadcasted_iota(jnp.int32, (rank, 2 * rank), 0)
    total = jnp.zeros((2 * rank, 2 * rank), F32)
    count = 0
    per_doc = []
    for doc in range(n_docs):
        in_proj = lax.dot_general(acts_v[doc], pin_v[...], NT, preferred_element_type=F32)
        out_proj = lax.dot_general(outg_v[doc], pout_v[...], NT, preferred_element_type=F32)
        both = jnp.concatenate([in_proj, out_proj], axis=1)
        size = lengths[doc]
        both = jnp.where(tokens < size, both, 0.0)
        gram = lax.dot_general(both, both, TN, precision=HIGHEST, preferred_element_type=F32)
        total = total + gram
        count = count + jnp.minimum(size, length)
        per_doc.append(gram[rank:, :rank] / size.astype(F32))
    packed = jnp.where(lanes < rank, total[:rank, :], total[rank:, :])
    counts = jnp.zeros((8, 2 * rank), F32) + count.astype(F32)
    for i in range(n_fsdp):
        piece = packed[i * share : (i + 1) * share, :]
        if share < 8:
            piece = jnp.concatenate([piece, jnp.zeros((8 - share, 2 * rank), F32)], axis=0)
        pieces[i, : piece.shape[0], :] = piece
        pieces[i, piece.shape[0] :, :] = counts

    def scatter_copy(d):
        return pltpu.make_async_remote_copy(
            src_ref=pieces.at[lax.rem(f + d, n_fsdp)], dst_ref=plane_slots.at[f],
            send_sem=ps.at[d], recv_sem=pr.at[d], device_id=in_plane(d), device_id_type=mesh_id)

    def column_copy(d):
        return pltpu.make_async_remote_copy(
            src_ref=column_slots.at[g], dst_ref=column_slots.at[g],
            send_sem=cs.at[d], recv_sem=cr.at[d], device_id=in_column(d), device_id_type=mesh_id)

    def total_copy(d):
        return pltpu.make_async_remote_copy(
            src_ref=totals.at[f], dst_ref=totals.at[f],
            send_sem=ts.at[d], recv_sem=tr.at[d], device_id=in_plane(d), device_id_type=mesh_id)

    block = 4 * rank
    eye = jnp.where(
        lax.broadcasted_iota(jnp.int32, (block, block), 0) == lax.broadcasted_iota(jnp.int32, (block, block), 1),
        1.0, 0.0).astype(BF16)

    def turn(e):
        unit = lax.rem(my_unit + n_units - e, n_units)
        unit_rows = pl.ds(pl.multiple_of(unit * UNIT, UNIT), UNIT)
        for i in range(width // block):
            chunk = raw[unit_rows, i * block : (i + 1) * block]
            part = lax.dot_general(eye, chunk, NT, preferred_element_type=F32)
            for a in range(4):
                start = (4 * i + a) * pitch
                work[0, start : start + rank, :] = part[a * rank : (a + 1) * rank, :]
        for b in range(rank):
            turned[unit, b * rank : (b + 1) * rank, :] = work[0, pl.ds(b, rank, stride=pitch), :].astype(BF16)

    def arrive(e):
        for i in range(unit_chips):
            if (e, i) != (0, 0):
                for p in range(cut):
                    shard_copy((e, i), p).wait()

    for d in range(1, n_fsdp):
        scatter_copy(d).start()
    send_part(1)
    plane_slots[f] = pieces[f]
    flat = [
        jnp.concatenate([grad[a : a + 1, :] for a in range(rank)], axis=1) for grad in per_doc
    ]
    fresh = jnp.concatenate(
        flat + [jnp.zeros((score_rows.shape[0] - stored - n_docs, width), F32)], axis=0).astype(BF16)
    score_rows[stored:, :] = fresh
    new_grads[...] = fresh[:n_docs]
    for d in range(1, n_fsdp):
        scatter_copy(d).wait()
    summed = plane_slots[0]
    for i in range(1, n_fsdp):
        summed = summed + plane_slots[i]
    column_slots[g] = summed
    for d in range(1, n_grp):
        column_copy(d).start()
    send_part(2)
    for d in range(1, n_grp):
        column_copy(d).wait()
    summed = column_slots[0]
    for i in range(1, n_grp):
        summed = summed + column_slots[i]
    totals[f] = summed
    for d in range(1, n_fsdp):
        total_copy(d).start()
    send_part(3)
    loads[4].wait()
    loads[5].wait()
    arrive(0)
    turn(0)
    for d in range(1, n_fsdp):
        total_copy(d).wait()

    covariance = jnp.concatenate([totals[i, :share, :] for i in range(n_fsdp)], axis=0)
    covariance = covariance / summed[summed.shape[0] - 1 :, :]
    diagonal = (rows == lanes) | (rows + rank == lanes)
    on_diagonal = jnp.where(diagonal, covariance, 0.0)
    in_trace = jnp.sum(jnp.where(lanes < rank, on_diagonal, 0.0))
    out_trace = jnp.sum(jnp.where(lanes < rank, 0.0, on_diagonal))
    ridge = jnp.where(lanes < rank, 0.1 * in_trace / rank, 0.1 * out_trace / rank)
    both = invert_pair(covariance + jnp.where(diagonal, ridge, 0.0), rank)

    ih, im, il = split3(both[:, :rank])
    zero = jnp.zeros((rank, rank), BF16)
    in_left = jnp.concatenate([
        jnp.concatenate([ih, ih, ih], axis=1),
        jnp.concatenate([im, im, zero], axis=1),
        jnp.concatenate([il, zero, zero], axis=1)], axis=0)
    out_left = jnp.concatenate(split3(both[:, rank:]), axis=0)

    for e in range(1, n_units):
        arrive(e)
        turn(e)

    for b in range(rank):
        right = jnp.concatenate([turned[u, b * rank : (b + 1) * rank, :] for u in range(n_units)], axis=1)
        part = jnp.dot(out_left, right, preferred_element_type=F32)
        part = part[:rank] + (part[rank : 2 * rank] + part[2 * rank :])
        for u in range(n_units):
            work[u, pl.ds(b, rank, stride=pitch), :] = part[:, u * UNIT : (u + 1) * UNIT]
    per_pass = rank // PASSES
    for a in range(rank):
        half_done = jnp.concatenate([work[u, a * pitch : a * pitch + rank, :] for u in range(n_units)], axis=1)
        right = jnp.concatenate(split3(half_done), axis=0)
        part = jnp.dot(in_left, right, preferred_element_type=F32)
        part = part[:rank] + (part[rank : 2 * rank] + part[2 * rank :])
        own[a * rank : (a + 1) * rank, :] = part.astype(BF16)
        if a % per_pass == per_pass - 1:
            pass_copy(a // per_pass).start()
    own_scores = jnp.dot(score_rows[...], own[...], preferred_element_type=F32).astype(BF16)
    for k in range(PASSES):
        pass_copy(k).wait()
    other_scores = jnp.dot(score_rows[...], other[...], preferred_element_type=F32).astype(BF16)
    scores = jnp.concatenate([own_scores, other_scores], axis=1)
    scores = jnp.dot(scores, order_m[...], preferred_element_type=F32).astype(BF16)
    store_out[...] = scores[:stored]
    new_out[...] = scores[stored : stored + n_docs]


PIECE = 16
UNIT = 128
AHEAD = 8
PASSES = 4
MARKS = (4, 6, 9)


def influence(n_grp, n_fsdp, doc_lengths, acts, out_grads, proj_in, proj_out, queries, store):
    n_docs = acts.shape[0]
    rank = proj_in.shape[0]
    here, width = queries.shape
    stored = store.shape[0]
    n_queries = n_fsdp * here
    dma = pltpu.SemaphoreType.DMA
    slot = (-(-(rank // n_fsdp) // 8) * 8 + 8, 2 * rank)
    score_rows = -(-(stored + n_docs) // 16) * 16
    copies = dma((n_fsdp // 2 * (here // PIECE),))
    mine = n_queries // 2
    return pl.pallas_call(
        functools.partial(influence_kernel, n_grp, n_fsdp),
        out_shape=(
            jax.ShapeDtypeStruct((n_docs, width), BF16),
            jax.ShapeDtypeStruct((stored, n_queries), BF16),
            jax.ShapeDtypeStruct((n_docs, n_queries), BF16),
        ),
        in_specs=[pl.BlockSpec(memory_space=pltpu.SMEM)] + [pl.BlockSpec(memory_space=ANY)] * 6,
        out_specs=tuple([pl.BlockSpec(memory_space=VMEM)] * 3),
        scratch_shapes=[
            VMEM(acts.shape, BF16), VMEM(out_grads.shape, BF16),
            VMEM(proj_in.shape, BF16), VMEM(proj_out.shape, BF16),
            VMEM((mine, width), BF16), VMEM((mine // UNIT, width, UNIT), BF16),
            VMEM((width, mine), BF16), VMEM((width, mine), BF16),
            VMEM((score_rows, width), BF16),
            VMEM((mine // UNIT, rank * (rank + 8), UNIT), F32),
            VMEM((n_queries, n_queries), BF16),
            VMEM((n_fsdp,) + slot, F32), VMEM((n_fsdp,) + slot, F32),
            VMEM((n_grp,) + slot, F32), VMEM((n_fsdp,) + slot, F32),
            dma((6,)), copies, copies, dma((PASSES,)), dma((PASSES,)),
            dma((n_fsdp,)), dma((n_fsdp,)), dma((n_grp,)), dma((n_grp,)), dma((n_fsdp,)), dma((n_fsdp,)),
        ],
        compiler_params=pltpu.CompilerParams(
            collective_id=0, has_side_effects=True, vmem_limit_bytes=60 * 2**20),
    )(doc_lengths, acts, out_grads, proj_in, proj_out, queries, store)


def solution(mesh):
    n_grp, n_fsdp = mesh.shape["grp"], mesh.shape["fsdp"]

    def shards(acts, out_grads, doc_lengths, proj_in, proj_out, store_grads, queries):
        return influence(
            n_grp, n_fsdp, doc_lengths, acts, out_grads, proj_in, proj_out, queries, store_grads)

    rows = P(("grp", "fsdp"), None)
    placed = (
        P(("grp", "fsdp"), None, None),
        P(("grp", "fsdp"), None, None),
        P(("grp", "fsdp")),
        P(),
        P(),
        rows,
        P("fsdp", None),
    )
    return jax.shard_map(
        shards, mesh=mesh, in_specs=placed, out_specs=(rows, rows, rows), check_vma=False)
```

```python
import functools

import jax
import jax.numpy as jnp
from jax import lax
from jax.experimental import pallas as pl
from jax.experimental.pallas import tpu as pltpu
from jax.sharding import PartitionSpec as P

F32 = jnp.float32
BF16 = jnp.bfloat16
ANY = pl.ANY
VMEM = pltpu.VMEM
HIGHEST = lax.Precision.HIGHEST
NT = (((1,), (1,)), ((), ()))
TN = (((0,), (0,)), ((), ()))


def invert_pair(matrix, rank):
    lanes = lax.broadcasted_iota(jnp.int32, (8, 2 * rank), 1)
    subs = lax.broadcasted_iota(jnp.int32, (8, 2 * rank), 0)
    left = lanes < rank
    local = jnp.where(left, lanes, lanes - rank)
    blocks = [matrix[i : i + 8, :] for i in range(0, rank, 8)]
    for first in range(0, rank, AHEAD):
        ahead = range(first, first + AHEAD)
        columns = [
            [jnp.take_along_axis(block, jnp.where(left, k, rank + k), axis=1) for block in blocks]
            for k in ahead
        ]
        for k in ahead:
            at, row = k // 8, k % 8
            column = columns[k - first]
            inverse_pivot = 1.0 / column[at][row : row + 1, :]
            at_pivot = local == k
            scaled = jnp.where(at_pivot[:1], 1.0, blocks[at][row : row + 1, :]) * inverse_pivot
            for later in range(k + 1 - first, AHEAD):
                part = columns[later][at][row : row + 1, :] * inverse_pivot
                reduced = [c - d * part for c, d in zip(columns[later], column)]
                reduced[at] = jnp.where(subs == row, part, reduced[at])
                columns[later] = reduced
            reduced = [jnp.where(at_pivot, 0.0, c) - d * scaled for c, d in zip(blocks, column)]
            reduced[at] = jnp.where(subs == row, scaled, reduced[at])
            blocks = reduced
    return jnp.concatenate(blocks, axis=0)


def split3(value):
    high = value.astype(BF16)
    rest = value - high.astype(F32)
    middle = rest.astype(BF16)
    low = (rest - middle.astype(F32)).astype(BF16)
    return high, middle, low


def send_order(n_units, per_unit, cut):
    steps = [(e, i) for e in range(n_units) for i in range(per_unit)][1:]
    order = []
    for p in range(cut):
        order.append(("cross", (0, 0), p))
        order.extend(("along", step, (p + cut // 2) % cut) for step in steps)
    for p in range(max(cut // 2, cut - cut // 2)):
        for step in steps:
            order.extend(("relay", step, q) for q in (p, cut // 2 + p) if p < cut // 2 or q == cut // 2 + p)
    return order


def influence_kernel(
    n_grp, n_fsdp,
    lengths, acts, out_grads, proj_in, proj_out, queries, store,
    new_grads, store_out, new_out,
    acts_v, outg_v, pin_v, pout_v, raw, turned, own, score_rows, work, order_m, lent, borrowed,
    pieces, plane_slots, column_slots, totals,
    load_sems, gs, gr, fs, fr, ps, pr, cs, cr, ts, tr,
):
    g = lax.axis_index("grp")
    f = lax.axis_index("fsdp")
    n_docs, length, features = acts.shape
    rank = proj_in.shape[0]
    here, width = queries.shape
    stored = store.shape[0]
    n_chips = n_fsdp // 2
    chip = f // 2
    core = lax.rem(f, 2)
    cut = here // PIECE
    share = rank // n_fsdp
    pitch = rank + 8
    spare = score_rows.shape[1] - stored
    mine = n_chips * here
    y = chip // 2
    x = lax.rem(chip, 2)
    per_unit = UNIT // here // 2
    n_units = n_chips // (UNIT // here)
    my_unit = y // per_unit
    my_place = lax.rem(y, per_unit)
    mesh_id = pl.DeviceIdType.MESH

    def in_plane(d):
        return {"grp": g, "fsdp": lax.rem(f + d, n_fsdp)}

    def in_column(d):
        return {"grp": lax.rem(g + d, n_grp), "fsdp": f}

    def rows_of(index, p):
        return raw.at[pl.ds(pl.multiple_of(index * here + p * PIECE, PIECE), PIECE)]

    def at(step, p, cross):
        return ((step[0] * per_unit + step[1]) * 2 + cross) * cut + p

    def moved(step, sign):
        unit = lax.rem(my_unit + n_units + sign * step[0], n_units)
        return unit * per_unit + lax.rem(my_place + per_unit + sign * step[1], per_unit)

    def block_copy(kind, step, p):
        across = (y * 2 + 1 - x) * 2 + core
        onward = (moved(step, 1) * 2 + x) * 2 + core
        if kind == "cross":
            source, target, where = chip, across, at((0, 0), p, 1)
        elif kind == "along":
            source, target, where = chip, onward, at(step, p, 0)
        elif p < cut // 2:
            source, target, where = y * 2 + 1 - x, onward, at(step, p, 1)
        else:
            source, target, where = moved(step, -1) * 2 + x, across, at(step, p, 1)
        rows = rows_of(source, p)
        return pltpu.make_async_remote_copy(
            src_ref=rows if kind == "relay" else queries.at[pl.ds(p * PIECE, PIECE)], dst_ref=rows_of(source, p),
            send_sem=gs.at[where], recv_sem=gr.at[where],
            device_id={"grp": g, "fsdp": target}, device_id_type=mesh_id)

    sibling = {"grp": g, "fsdp": f + 1 - 2 * core}

    def pass_copy(k):
        ends = (
            (store, score_rows.at[1, pl.ds(0, stored)]),
            (score_rows.at[0, pl.ds(stored, spare)], score_rows.at[1, pl.ds(stored, spare)]),
        ) + tuple((lent.at[e], borrowed.at[e]) for e in range(n_units))
        return pltpu.make_async_remote_copy(
            src_ref=ends[k][0], dst_ref=ends[k][1], send_sem=fs.at[k], recv_sem=fr.at[k],
            device_id=sibling, device_id_type=mesh_id)

    own_rows = raw.at[pl.ds(pl.multiple_of(chip * here, here), here)]
    loads = [
        pltpu.make_async_copy(src, dst, load_sems.at[i])
        for i, (src, dst) in enumerate((
            (acts, acts_v), (proj_in, pin_v), (out_grads, outg_v), (proj_out, pout_v),
            (queries, own_rows), (store, score_rows.at[0, pl.ds(0, stored)])))
    ]
    for load in loads:
        load.start()

    barrier = pltpu.get_barrier_semaphore()

    def greet_plane(d, _):
        pl.semaphore_signal(barrier, inc=1, device_id=in_plane(d), device_id_type=mesh_id)
        return 0

    def greet_column(d, _):
        pl.semaphore_signal(barrier, inc=1, device_id=in_column(d), device_id_type=mesh_id)
        return 0

    lax.fori_loop(1, n_fsdp, greet_plane, 0)
    lax.fori_loop(1, n_grp, greet_column, 0)

    wide_row = lax.broadcasted_iota(jnp.int32, order_m.shape, 0)
    wide_lane = lax.broadcasted_iota(jnp.int32, order_m.shape, 1)
    from_core = lax.rem(wide_lane // here, 2)
    from_unit = lax.rem(my_unit + n_units - wide_lane // (2 * UNIT), n_units)
    from_row = (
        jnp.where(from_core == core, 0, mine) + from_unit * UNIT
        + lax.rem(wide_lane // (2 * here), UNIT // here) * here + lax.rem(wide_lane, here))
    order_m[...] = jnp.where(wide_row == from_row, 1.0, 0.0).astype(BF16)

    order = send_order(n_units, per_unit, cut)
    marks = [0] + [len(order) * m // 12 for m in MARKS] + [len(order)]
    landed = set()

    def land(kind, step, p):
        if (kind, step, p) not in landed:
            landed.add((kind, step, p))
            block_copy(kind, step, p).wait_recv()

    def send_part(j):
        for kind, step, p in order[marks[j] : marks[j + 1]]:
            if kind == "relay":
                if p < cut // 2:
                    land("cross", (0, 0), p)
                else:
                    land("along", step, p)
            block_copy(kind, step, p).start()

    pl.semaphore_wait(barrier, n_fsdp - 1 + n_grp - 1)
    send_part(0)
    pass_copy(0).start()
    for load in loads[:4]:
        load.wait()

    tokens = lax.broadcasted_iota(jnp.int32, (length, 2 * rank), 0)
    lanes = lax.broadcasted_iota(jnp.int32, (rank, 2 * rank), 1)
    rows = lax.broadcasted_iota(jnp.int32, (rank, 2 * rank), 0)
    total = jnp.zeros((2 * rank, 2 * rank), F32)
    count = 0
    per_doc = []
    for doc in range(n_docs):
        in_proj = lax.dot_general(acts_v[doc], pin_v[...], NT, preferred_element_type=F32)
        out_proj = lax.dot_general(outg_v[doc], pout_v[...], NT, preferred_element_type=F32)
        both = jnp.concatenate([in_proj, out_proj], axis=1)
        size = lengths[doc]
        both = jnp.where(tokens < size, both, 0.0)
        gram = lax.dot_general(both, both, TN, precision=HIGHEST, preferred_element_type=F32)
        total = total + gram
        count = count + jnp.minimum(size, length)
        per_doc.append(gram[rank:, :rank] / size.astype(F32))
    packed = jnp.where(lanes < rank, total[:rank, :], total[rank:, :])
    counts = jnp.zeros((8, 2 * rank), F32) + count.astype(F32)
    for i in range(n_fsdp):
        piece = packed[i * share : (i + 1) * share, :]
        if share < 8:
            piece = jnp.concatenate([piece, jnp.zeros((8 - share, 2 * rank), F32)], axis=0)
        pieces[i, : piece.shape[0], :] = piece
        pieces[i, piece.shape[0] :, :] = counts

    def scatter_copy(d):
        return pltpu.make_async_remote_copy(
            src_ref=pieces.at[lax.rem(f + d, n_fsdp)], dst_ref=plane_slots.at[f],
            send_sem=ps.at[d], recv_sem=pr.at[d], device_id=in_plane(d), device_id_type=mesh_id)

    def column_copy(d):
        return pltpu.make_async_remote_copy(
            src_ref=column_slots.at[g], dst_ref=column_slots.at[g],
            send_sem=cs.at[d], recv_sem=cr.at[d], device_id=in_column(d), device_id_type=mesh_id)

    def total_copy(d):
        return pltpu.make_async_remote_copy(
            src_ref=totals.at[f], dst_ref=totals.at[f],
            send_sem=ts.at[d], recv_sem=tr.at[d], device_id=in_plane(d), device_id_type=mesh_id)

    block = 4 * rank
    eye = jnp.where(
        lax.broadcasted_iota(jnp.int32, (block, block), 0) == lax.broadcasted_iota(jnp.int32, (block, block), 1),
        1.0, 0.0).astype(BF16)

    def turn(e):
        unit = lax.rem(my_unit + n_units - e, n_units)
        unit_rows = pl.ds(pl.multiple_of(unit * UNIT, UNIT), UNIT)
        for i in range(width // block):
            chunk = raw[unit_rows, i * block : (i + 1) * block]
            part = lax.dot_general(eye, chunk, NT, preferred_element_type=F32)
            for a in range(4):
                start = (4 * i + a) * pitch
                work[0, start : start + rank, :] = part[a * rank : (a + 1) * rank, :]
        for b in range(rank):
            turned[e, b * rank : (b + 1) * rank, :] = work[0, pl.ds(b, rank, stride=pitch), :].astype(BF16)

    def arrive(e):
        for kind, step, p in order:
            if step[0] == e:
                land(kind, step, p)

    for d in range(1, n_fsdp):
        scatter_copy(d).start()
    send_part(1)
    plane_slots[f] = pieces[f]
    flat = [
        jnp.concatenate([grad[a : a + 1, :] for a in range(rank)], axis=1) for grad in per_doc
    ]
    fresh = jnp.concatenate(
        flat + [jnp.zeros((spare - n_docs, width), F32)], axis=0).astype(BF16)
    score_rows[0, stored:, :] = fresh
    pass_copy(1).start()
    new_grads[...] = fresh[:n_docs]
    for d in range(1, n_fsdp):
        scatter_copy(d).wait()
    summed = plane_slots[0]
    for i in range(1, n_fsdp):
        summed = summed + plane_slots[i]
    column_slots[g] = summed
    for d in range(1, n_grp):
        column_copy(d).start()
    send_part(2)
    for d in range(1, n_grp):
        column_copy(d).wait()
    summed = column_slots[0]
    for i in range(1, n_grp):
        summed = summed + column_slots[i]
    totals[f] = summed
    for d in range(1, n_fsdp):
        total_copy(d).start()
    send_part(3)
    loads[4].wait()
    loads[5].wait()
    arrive(0)
    turn(0)
    for d in range(1, n_fsdp):
        total_copy(d).wait()

    covariance = jnp.concatenate([totals[i, :share, :] for i in range(n_fsdp)], axis=0)
    covariance = covariance / summed[summed.shape[0] - 1 :, :]
    diagonal = (rows == lanes) | (rows + rank == lanes)
    on_diagonal = jnp.where(diagonal, covariance, 0.0)
    in_trace = jnp.sum(jnp.where(lanes < rank, on_diagonal, 0.0))
    out_trace = jnp.sum(jnp.where(lanes < rank, 0.0, on_diagonal))
    ridge = jnp.where(lanes < rank, 0.1 * in_trace / rank, 0.1 * out_trace / rank)
    both = invert_pair(covariance + jnp.where(diagonal, ridge, 0.0), rank)

    ih, im, il = split3(both[:, :rank])
    zero = jnp.zeros((rank, rank), BF16)
    in_left = jnp.concatenate([
        jnp.concatenate([ih, ih, ih], axis=1),
        jnp.concatenate([im, im, zero], axis=1),
        jnp.concatenate([il, zero, zero], axis=1)], axis=0)
    out_left = jnp.concatenate(split3(both[:, rank:]), axis=0)

    pass_copy(0).wait()
    pass_copy(1).wait()
    own_scores = []
    for e in range(n_units):
        if e:
            arrive(e)
            turn(e)
        for b in range(rank):
            part = jnp.dot(out_left, turned[e, b * rank : (b + 1) * rank, :], preferred_element_type=F32)
            part = part[:rank] + (part[rank : 2 * rank] + part[2 * rank :])
            work[e, pl.ds(b, rank, stride=pitch), :] = part
        for a in range(rank):
            right = jnp.concatenate(split3(work[e, a * pitch : a * pitch + rank, :]), axis=0)
            part = jnp.dot(in_left, right, preferred_element_type=F32)
            part = part[:rank] + (part[rank : 2 * rank] + part[2 * rank :])
            own[e, a * rank : (a + 1) * rank, :] = part.astype(BF16)
        lent[e] = jnp.dot(score_rows[1], own[e], preferred_element_type=F32).astype(BF16)
        pass_copy(2 + e).start()
        own_scores.append(jnp.dot(score_rows[0], own[e], preferred_element_type=F32).astype(BF16))
    for e in range(n_units):
        pass_copy(2 + e).wait()
    scores = jnp.concatenate(own_scores + [borrowed[e] for e in range(n_units)], axis=1)
    scores = jnp.dot(scores, order_m[...], preferred_element_type=F32).astype(BF16)
    for kind, step, p in order:
        block_copy(kind, step, p).wait_send()
    store_out[...] = scores[:stored]
    new_out[...] = scores[stored : stored + n_docs]


PIECE = 16
UNIT = 128
AHEAD = 8
MARKS = (4, 6, 9)


def hand_over(*refs):
    for source, target in zip(refs[:3], refs[3:]):
        target[...] = source[...]


def influence(n_grp, n_fsdp, doc_lengths, acts, out_grads, proj_in, proj_out, queries, store):
    n_docs = acts.shape[0]
    rank = proj_in.shape[0]
    here, width = queries.shape
    stored = store.shape[0]
    n_queries = n_fsdp * here
    dma = pltpu.SemaphoreType.DMA
    slot = (-(-(rank // n_fsdp) // 8) * 8 + 8, 2 * rank)
    score_rows = -(-(stored + n_docs) // 16) * 16
    copies = dma((n_fsdp // 2 * (here // PIECE),))
    mine = n_queries // 2
    results = pl.pallas_call(
        functools.partial(influence_kernel, n_grp, n_fsdp),
        out_shape=(
            VMEM((n_docs, width), BF16),
            VMEM((stored, n_queries), BF16),
            VMEM((n_docs, n_queries), BF16),
        ),
        in_specs=[pl.BlockSpec(memory_space=pltpu.SMEM)] + [pl.BlockSpec(memory_space=ANY)] * 6,
        out_specs=tuple([pl.BlockSpec(memory_space=VMEM)] * 3),
        scratch_shapes=[
            VMEM(acts.shape, BF16), VMEM(out_grads.shape, BF16),
            VMEM(proj_in.shape, BF16), VMEM(proj_out.shape, BF16),
            VMEM((mine, width), BF16), VMEM((mine // UNIT, width, UNIT), BF16),
            VMEM((mine // UNIT, width, UNIT), BF16), VMEM((2, score_rows, width), BF16),
            VMEM((mine // UNIT, rank * (rank + 8), UNIT), F32),
            VMEM((n_queries, n_queries), BF16),
            VMEM((mine // UNIT, score_rows, UNIT), BF16), VMEM((mine // UNIT, score_rows, UNIT), BF16),
            VMEM((n_fsdp,) + slot, F32), VMEM((n_fsdp,) + slot, F32),
            VMEM((n_grp,) + slot, F32), VMEM((n_fsdp,) + slot, F32),
            dma((6,)), copies, copies, dma((2 + mine // UNIT,)), dma((2 + mine // UNIT,)),
            dma((n_fsdp,)), dma((n_fsdp,)), dma((n_grp,)), dma((n_grp,)), dma((n_fsdp,)), dma((n_fsdp,)),
        ],
        compiler_params=pltpu.CompilerParams(
            collective_id=0, has_side_effects=True, vmem_limit_bytes=56 * 2**20),
    )(doc_lengths, acts, out_grads, proj_in, proj_out, queries, store)
    return pl.pallas_call(
        hand_over,
        out_shape=tuple(jax.ShapeDtypeStruct(r.shape, r.dtype) for r in results),
        in_specs=[pl.BlockSpec(memory_space=VMEM)] * 3,
        out_specs=tuple([pl.BlockSpec(memory_space=VMEM)] * 3),
        compiler_params=pltpu.CompilerParams(vmem_limit_bytes=4 * 2**20),
    )(*results)


def solution(mesh):
    n_grp, n_fsdp = mesh.shape["grp"], mesh.shape["fsdp"]

    def shards(acts, out_grads, doc_lengths, proj_in, proj_out, store_grads, queries):
        return influence(
            n_grp, n_fsdp, doc_lengths, acts, out_grads, proj_in, proj_out, queries, store_grads)

    rows = P(("grp", "fsdp"), None)
    placed = (
        P(("grp", "fsdp"), None, None),
        P(("grp", "fsdp"), None, None),
        P(("grp", "fsdp")),
        P(),
        P(),
        rows,
        P("fsdp", None),
    )
    return jax.shard_map(
        shards, mesh=mesh, in_specs=placed, out_specs=(rows, rows, rows), check_vma=False)
```

```python
import functools

import jax
import jax.numpy as jnp
from jax import lax
from jax.experimental import pallas as pl
from jax.experimental.pallas import tpu as pltpu
from jax.sharding import PartitionSpec as P

F32 = jnp.float32
BF16 = jnp.bfloat16
ANY = pl.ANY
VMEM = pltpu.VMEM
HIGHEST = lax.Precision.HIGHEST
NT = (((1,), (1,)), ((), ()))
TN = (((0,), (0,)), ((), ()))


def invert_pair(matrix, rank):
    lanes = lax.broadcasted_iota(jnp.int32, (8, 2 * rank), 1)
    subs = lax.broadcasted_iota(jnp.int32, (8, 2 * rank), 0)
    left = lanes < rank
    local = jnp.where(left, lanes, lanes - rank)
    blocks = [matrix[i : i + 8, :] for i in range(0, rank, 8)]
    for first in range(0, rank, AHEAD):
        ahead = range(first, first + AHEAD)
        columns = [
            [jnp.take_along_axis(block, jnp.where(left, k, rank + k), axis=1) for block in blocks]
            for k in ahead
        ]
        for k in ahead:
            at, row = k // 8, k % 8
            column = columns[k - first]
            inverse_pivot = 1.0 / column[at][row : row + 1, :]
            at_pivot = local == k
            scaled = jnp.where(at_pivot[:1], 1.0, blocks[at][row : row + 1, :]) * inverse_pivot
            for later in range(k + 1 - first, AHEAD):
                part = columns[later][at][row : row + 1, :] * inverse_pivot
                reduced = [c - d * part for c, d in zip(columns[later], column)]
                reduced[at] = jnp.where(subs == row, part, reduced[at])
                columns[later] = reduced
            reduced = [jnp.where(at_pivot, 0.0, c) - d * scaled for c, d in zip(blocks, column)]
            reduced[at] = jnp.where(subs == row, scaled, reduced[at])
            blocks = reduced
    return jnp.concatenate(blocks, axis=0)


def split3(value):
    high = value.astype(BF16)
    rest = value - high.astype(F32)
    middle = rest.astype(BF16)
    low = (rest - middle.astype(F32)).astype(BF16)
    return high, middle, low


def send_order(n_units, per_unit, cut):
    steps = [(e, i) for e in range(n_units) for i in range(per_unit)][1:]
    order = []
    for p in range(cut):
        order.append(("cross", (0, 0), p))
        order.extend(("along", step, (p + cut // 2) % cut) for step in steps)
    for p in range(max(cut // 2, cut - cut // 2)):
        for step in steps:
            order.extend(("relay", step, q) for q in (p, cut // 2 + p) if p < cut // 2 or q == cut // 2 + p)
    return order


def influence_kernel(
    n_grp, n_fsdp,
    lengths, acts, out_grads, proj_in, proj_out, queries, store,
    new_grads, store_out, new_out,
    acts_v, outg_v, pin_v, pout_v, raw, turned, own, score_rows, work, order_m, lent, borrowed,
    pieces, plane_slots, column_slots, totals,
    load_sems, gs, gr, fs, fr, ps, pr, cs, cr, ts, tr,
):
    g = lax.axis_index("grp")
    f = lax.axis_index("fsdp")
    n_docs, length, features = acts.shape
    rank = proj_in.shape[0]
    here, width = queries.shape
    stored = store.shape[0]
    n_chips = n_fsdp // 2
    chip = f // 2
    core = lax.rem(f, 2)
    cut = here // PIECE
    share = rank // n_fsdp
    pitch = rank + 8
    spare = score_rows.shape[1] - stored
    mine = n_chips * here
    y = chip // 2
    x = lax.rem(chip, 2)
    per_unit = UNIT // here // 2
    n_units = n_chips // (UNIT // here)
    my_unit = y // per_unit
    my_place = lax.rem(y, per_unit)
    mesh_id = pl.DeviceIdType.MESH

    def in_plane(d):
        return {"grp": g, "fsdp": lax.rem(f + d, n_fsdp)}

    def in_column(d):
        return {"grp": lax.rem(g + d, n_grp), "fsdp": f}

    def rows_of(index, p):
        return raw.at[pl.ds(pl.multiple_of(index * here + p * PIECE, PIECE), PIECE)]

    def at(step, p, cross):
        return ((step[0] * per_unit + step[1]) * 2 + cross) * cut + p

    def moved(step, sign):
        unit = lax.rem(my_unit + n_units + sign * step[0], n_units)
        return unit * per_unit + lax.rem(my_place + per_unit + sign * step[1], per_unit)

    def block_copy(kind, step, p):
        across = (y * 2 + 1 - x) * 2 + core
        onward = (moved(step, 1) * 2 + x) * 2 + core
        if kind == "cross":
            source, target, where = chip, across, at((0, 0), p, 1)
        elif kind == "along":
            source, target, where = chip, onward, at(step, p, 0)
        elif p < cut // 2:
            source, target, where = y * 2 + 1 - x, onward, at(step, p, 1)
        else:
            source, target, where = moved(step, -1) * 2 + x, across, at(step, p, 1)
        rows = rows_of(source, p)
        return pltpu.make_async_remote_copy(
            src_ref=rows if kind == "relay" else queries.at[pl.ds(p * PIECE, PIECE)], dst_ref=rows_of(source, p),
            send_sem=gs.at[where], recv_sem=gr.at[where],
            device_id={"grp": g, "fsdp": target}, device_id_type=mesh_id)

    sibling = {"grp": g, "fsdp": f + 1 - 2 * core}

    def pass_copy(k):
        ends = (
            (store, score_rows.at[1, pl.ds(0, stored)]),
            (score_rows.at[0, pl.ds(stored, spare)], score_rows.at[1, pl.ds(stored, spare)]),
        ) + tuple((lent.at[e], borrowed.at[e]) for e in range(n_units))
        return pltpu.make_async_remote_copy(
            src_ref=ends[k][0], dst_ref=ends[k][1], send_sem=fs.at[k], recv_sem=fr.at[k],
            device_id=sibling, device_id_type=mesh_id)

    own_rows = raw.at[pl.ds(pl.multiple_of(chip * here, here), here)]
    loads = [
        pltpu.make_async_copy(src, dst, load_sems.at[i])
        for i, (src, dst) in enumerate((
            (acts, acts_v), (proj_in, pin_v), (out_grads, outg_v), (proj_out, pout_v),
            (queries, own_rows), (store, score_rows.at[0, pl.ds(0, stored)])))
    ]
    for load in loads:
        load.start()

    barrier = pltpu.get_barrier_semaphore()

    def greet_plane(d, _):
        pl.semaphore_signal(barrier, inc=1, device_id=in_plane(d), device_id_type=mesh_id)
        return 0

    def greet_column(d, _):
        pl.semaphore_signal(barrier, inc=1, device_id=in_column(d), device_id_type=mesh_id)
        return 0

    lax.fori_loop(1, n_fsdp, greet_plane, 0)
    lax.fori_loop(1, n_grp, greet_column, 0)

    order = send_order(n_units, per_unit, cut)
    marks = [0] + [len(order) * m // 12 for m in MARKS] + [len(order)]
    landed = set()

    def land(kind, step, p):
        if (kind, step, p) not in landed:
            landed.add((kind, step, p))
            block_copy(kind, step, p).wait_recv()

    def send_part(j):
        for kind, step, p in order[marks[j] : marks[j + 1]]:
            if kind == "relay":
                if p < cut // 2:
                    land("cross", (0, 0), p)
                else:
                    land("along", step, p)
            block_copy(kind, step, p).start()

    for load in loads[:4]:
        load.wait()

    tokens = lax.broadcasted_iota(jnp.int32, (length, 2 * rank), 0)
    lanes = lax.broadcasted_iota(jnp.int32, (rank, 2 * rank), 1)
    rows = lax.broadcasted_iota(jnp.int32, (rank, 2 * rank), 0)
    total = jnp.zeros((2 * rank, 2 * rank), F32)
    count = 0
    per_doc = []
    for doc in range(n_docs):
        in_proj = lax.dot_general(acts_v[doc], pin_v[...], NT, preferred_element_type=F32)
        out_proj = lax.dot_general(outg_v[doc], pout_v[...], NT, preferred_element_type=F32)
        both = jnp.concatenate([in_proj, out_proj], axis=1)
        size = lengths[doc]
        both = jnp.where(tokens < size, both, 0.0)
        gram = lax.dot_general(both, both, TN, precision=HIGHEST, preferred_element_type=F32)
        total = total + gram
        count = count + jnp.minimum(size, length)
        per_doc.append(gram[rank:, :rank] / size.astype(F32))
    packed = jnp.where(lanes < rank, total[:rank, :], total[rank:, :])
    counts = jnp.zeros((8, 2 * rank), F32) + count.astype(F32)
    for i in range(n_fsdp):
        piece = packed[i * share : (i + 1) * share, :]
        if share < 8:
            piece = jnp.concatenate([piece, jnp.zeros((8 - share, 2 * rank), F32)], axis=0)
        pieces[i, : piece.shape[0], :] = piece
        pieces[i, piece.shape[0] :, :] = counts

    def scatter_copy(d):
        return pltpu.make_async_remote_copy(
            src_ref=pieces.at[lax.rem(f + d, n_fsdp)], dst_ref=plane_slots.at[f],
            send_sem=ps.at[d], recv_sem=pr.at[d], device_id=in_plane(d), device_id_type=mesh_id)

    def column_copy(d):
        return pltpu.make_async_remote_copy(
            src_ref=column_slots.at[g], dst_ref=column_slots.at[g],
            send_sem=cs.at[d], recv_sem=cr.at[d], device_id=in_column(d), device_id_type=mesh_id)

    def total_copy(d):
        return pltpu.make_async_remote_copy(
            src_ref=totals.at[f], dst_ref=totals.at[f],
            send_sem=ts.at[d], recv_sem=tr.at[d], device_id=in_plane(d), device_id_type=mesh_id)

    block = 4 * rank
    eye = jnp.where(
        lax.broadcasted_iota(jnp.int32, (block, block), 0) == lax.broadcasted_iota(jnp.int32, (block, block), 1),
        1.0, 0.0).astype(BF16)

    def turn(e):
        unit = lax.rem(my_unit + n_units - e, n_units)
        unit_rows = pl.ds(pl.multiple_of(unit * UNIT, UNIT), UNIT)
        for i in range(width // block):
            chunk = raw[unit_rows, i * block : (i + 1) * block]
            part = lax.dot_general(eye, chunk, NT, preferred_element_type=F32)
            for a in range(4):
                start = (4 * i + a) * pitch
                work[0, start : start + rank, :] = part[a * rank : (a + 1) * rank, :]
        for b in range(rank):
            turned[e, b * rank : (b + 1) * rank, :] = work[0, pl.ds(b, rank, stride=pitch), :].astype(BF16)

    def arrive(e):
        for kind, step, p in order:
            if step[0] == e:
                land(kind, step, p)

    pl.semaphore_wait(barrier, n_fsdp - 1 + n_grp - 1)
    for d in range(1, n_fsdp):
        scatter_copy(d).start()
    send_part(0)
    pass_copy(0).start()
    plane_slots[f] = pieces[f]
    flat = [
        jnp.concatenate([grad[a : a + 1, :] for a in range(rank)], axis=1) for grad in per_doc
    ]
    fresh = jnp.concatenate(
        flat + [jnp.zeros((spare - n_docs, width), F32)], axis=0).astype(BF16)
    score_rows[0, stored:, :] = fresh
    pass_copy(1).start()
    new_grads[...] = fresh[:n_docs]
    for d in range(1, n_fsdp):
        scatter_copy(d).wait()
    summed = plane_slots[0]
    for i in range(1, n_fsdp):
        summed = summed + plane_slots[i]
    column_slots[g] = summed
    for d in range(1, n_grp):
        column_copy(d).start()
    send_part(1)
    for d in range(1, n_grp):
        column_copy(d).wait()
    summed = column_slots[0]
    for i in range(1, n_grp):
        summed = summed + column_slots[i]
    totals[f] = summed
    for d in range(1, n_fsdp):
        total_copy(d).start()
    send_part(2)
    wide_row = lax.broadcasted_iota(jnp.int32, order_m.shape, 0)
    wide_lane = lax.broadcasted_iota(jnp.int32, order_m.shape, 1)
    from_core = lax.rem(wide_lane // here, 2)
    from_unit = lax.rem(my_unit + n_units - wide_lane // (2 * UNIT), n_units)
    from_row = (
        jnp.where(from_core == core, 0, mine) + from_unit * UNIT
        + lax.rem(wide_lane // (2 * here), UNIT // here) * here + lax.rem(wide_lane, here))
    order_m[...] = jnp.where(wide_row == from_row, 1.0, 0.0).astype(BF16)

    loads[4].wait()
    loads[5].wait()
    arrive(0)
    turn(0)
    for d in range(1, n_fsdp):
        total_copy(d).wait()

    covariance = jnp.concatenate([totals[i, :share, :] for i in range(n_fsdp)], axis=0)
    covariance = covariance / summed[summed.shape[0] - 1 :, :]
    diagonal = (rows == lanes) | (rows + rank == lanes)
    on_diagonal = jnp.where(diagonal, covariance, 0.0)
    in_trace = jnp.sum(jnp.where(lanes < rank, on_diagonal, 0.0))
    out_trace = jnp.sum(jnp.where(lanes < rank, 0.0, on_diagonal))
    ridge = jnp.where(lanes < rank, 0.1 * in_trace / rank, 0.1 * out_trace / rank)
    both = invert_pair(covariance + jnp.where(diagonal, ridge, 0.0), rank)

    ih, im, il = split3(both[:, :rank])
    zero = jnp.zeros((rank, rank), BF16)
    in_left = jnp.concatenate([
        jnp.concatenate([ih, ih, ih], axis=1),
        jnp.concatenate([im, im, zero], axis=1),
        jnp.concatenate([il, zero, zero], axis=1)], axis=0)
    out_left = jnp.concatenate(split3(both[:, rank:]), axis=0)

    pass_copy(0).wait()
    pass_copy(1).wait()
    own_scores = []
    for e in range(n_units):
        if e:
            arrive(e)
            turn(e)
        for b in range(rank):
            part = jnp.dot(out_left, turned[e, b * rank : (b + 1) * rank, :], preferred_element_type=F32)
            part = part[:rank] + (part[rank : 2 * rank] + part[2 * rank :])
            work[e, pl.ds(b, rank, stride=pitch), :] = part
        for a in range(rank):
            right = jnp.concatenate(split3(work[e, a * pitch : a * pitch + rank, :]), axis=0)
            part = jnp.dot(in_left, right, preferred_element_type=F32)
            part = part[:rank] + (part[rank : 2 * rank] + part[2 * rank :])
            own[e, a * rank : (a + 1) * rank, :] = part.astype(BF16)
        lent[e] = jnp.dot(score_rows[1], own[e], preferred_element_type=F32).astype(BF16)
        pass_copy(2 + e).start()
        own_scores.append(jnp.dot(score_rows[0], own[e], preferred_element_type=F32).astype(BF16))
    for e in range(n_units):
        pass_copy(2 + e).wait()
    scores = jnp.concatenate(own_scores + [borrowed[e] for e in range(n_units)], axis=1)
    scores = jnp.dot(scores, order_m[...], preferred_element_type=F32).astype(BF16)
    for kind, step, p in order:
        block_copy(kind, step, p).wait_send()
    store_out[...] = scores[:stored]
    new_out[...] = scores[stored : stored + n_docs]


PIECE = 16
UNIT = 128
AHEAD = 8
MARKS = (4, 8)


def hand_over(*refs):
    for source, target in zip(refs[:3], refs[3:]):
        target[...] = source[...]


def influence(n_grp, n_fsdp, doc_lengths, acts, out_grads, proj_in, proj_out, queries, store):
    n_docs = acts.shape[0]
    rank = proj_in.shape[0]
    here, width = queries.shape
    stored = store.shape[0]
    n_queries = n_fsdp * here
    dma = pltpu.SemaphoreType.DMA
    slot = (-(-(rank // n_fsdp) // 8) * 8 + 8, 2 * rank)
    score_rows = -(-(stored + n_docs) // 16) * 16
    copies = dma((n_fsdp // 2 * (here // PIECE),))
    mine = n_queries // 2
    results = pl.pallas_call(
        functools.partial(influence_kernel, n_grp, n_fsdp),
        out_shape=(
            VMEM((n_docs, width), BF16),
            VMEM((stored, n_queries), BF16),
            VMEM((n_docs, n_queries), BF16),
        ),
        in_specs=[pl.BlockSpec(memory_space=pltpu.SMEM)] + [pl.BlockSpec(memory_space=ANY)] * 6,
        out_specs=tuple([pl.BlockSpec(memory_space=VMEM)] * 3),
        scratch_shapes=[
            VMEM(acts.shape, BF16), VMEM(out_grads.shape, BF16),
            VMEM(proj_in.shape, BF16), VMEM(proj_out.shape, BF16),
            VMEM((mine, width), BF16), VMEM((mine // UNIT, width, UNIT), BF16),
            VMEM((mine // UNIT, width, UNIT), BF16), VMEM((2, score_rows, width), BF16),
            VMEM((mine // UNIT, rank * (rank + 8), UNIT), F32),
            VMEM((n_queries, n_queries), BF16),
            VMEM((mine // UNIT, score_rows, UNIT), BF16), VMEM((mine // UNIT, score_rows, UNIT), BF16),
            VMEM((n_fsdp,) + slot, F32), VMEM((n_fsdp,) + slot, F32),
            VMEM((n_grp,) + slot, F32), VMEM((n_fsdp,) + slot, F32),
            dma((6,)), copies, copies, dma((2 + mine // UNIT,)), dma((2 + mine // UNIT,)),
            dma((n_fsdp,)), dma((n_fsdp,)), dma((n_grp,)), dma((n_grp,)), dma((n_fsdp,)), dma((n_fsdp,)),
        ],
        compiler_params=pltpu.CompilerParams(
            collective_id=0, has_side_effects=True, vmem_limit_bytes=56 * 2**20),
    )(doc_lengths, acts, out_grads, proj_in, proj_out, queries, store)
    return pl.pallas_call(
        hand_over,
        out_shape=tuple(jax.ShapeDtypeStruct(r.shape, r.dtype) for r in results),
        in_specs=[pl.BlockSpec(memory_space=VMEM)] * 3,
        out_specs=tuple([pl.BlockSpec(memory_space=VMEM)] * 3),
        compiler_params=pltpu.CompilerParams(vmem_limit_bytes=4 * 2**20),
    )(*results)


def solution(mesh):
    n_grp, n_fsdp = mesh.shape["grp"], mesh.shape["fsdp"]

    def shards(acts, out_grads, doc_lengths, proj_in, proj_out, store_grads, queries):
        return influence(
            n_grp, n_fsdp, doc_lengths, acts, out_grads, proj_in, proj_out, queries, store_grads)

    rows = P(("grp", "fsdp"), None)
    placed = (
        P(("grp", "fsdp"), None, None),
        P(("grp", "fsdp"), None, None),
        P(("grp", "fsdp")),
        P(),
        P(),
        rows,
        P("fsdp", None),
    )
    return jax.shard_map(
        shards, mesh=mesh, in_specs=placed, out_specs=(rows, rows, rows), check_vma=False)
```

```python
import functools

import jax
import jax.numpy as jnp
from jax import lax
from jax.experimental import pallas as pl
from jax.experimental.pallas import tpu as pltpu
from jax.sharding import PartitionSpec as P

F32 = jnp.float32
BF16 = jnp.bfloat16
ANY = pl.ANY
VMEM = pltpu.VMEM
HIGHEST = lax.Precision.HIGHEST
NT = (((1,), (1,)), ((), ()))
TN = (((0,), (0,)), ((), ()))


def invert_pair(matrix, rank):
    lanes = lax.broadcasted_iota(jnp.int32, (8, 2 * rank), 1)
    subs = lax.broadcasted_iota(jnp.int32, (8, 2 * rank), 0)
    left = lanes < rank
    local = jnp.where(left, lanes, lanes - rank)
    blocks = [matrix[i : i + 8, :] for i in range(0, rank, 8)]
    for first in range(0, rank, AHEAD):
        ahead = range(first, first + AHEAD)
        columns = [
            [jnp.take_along_axis(block, jnp.where(left, k, rank + k), axis=1) for block in blocks]
            for k in ahead
        ]
        for k in ahead:
            at, row = k // 8, k % 8
            column = columns[k - first]
            inverse_pivot = 1.0 / column[at][row : row + 1, :]
            at_pivot = local == k
            scaled = jnp.where(at_pivot[:1], 1.0, blocks[at][row : row + 1, :]) * inverse_pivot
            for later in range(k + 1 - first, AHEAD):
                part = columns[later][at][row : row + 1, :] * inverse_pivot
                reduced = [c - d * part for c, d in zip(columns[later], column)]
                reduced[at] = jnp.where(subs == row, part, reduced[at])
                columns[later] = reduced
            reduced = [jnp.where(at_pivot, 0.0, c) - d * scaled for c, d in zip(blocks, column)]
            reduced[at] = jnp.where(subs == row, scaled, reduced[at])
            blocks = reduced
    return jnp.concatenate(blocks, axis=0)


def split3(value):
    high = value.astype(BF16)
    rest = value - high.astype(F32)
    middle = rest.astype(BF16)
    low = (rest - middle.astype(F32)).astype(BF16)
    return high, middle, low


def send_order(n_units, per_unit, cut):
    steps = [(e, i) for e in range(n_units) for i in range(per_unit)][1:]
    order = []
    for p in range(cut):
        order.append(("cross", (0, 0), p))
        order.extend(("along", step, (p + cut // 2) % cut) for step in steps)
    for p in range(max(cut // 2, cut - cut // 2)):
        for step in steps:
            order.extend(("relay", step, q) for q in (p, cut // 2 + p) if p < cut // 2 or q == cut // 2 + p)
    return order


def influence_kernel(
    n_grp, n_fsdp,
    lengths, acts, out_grads, proj_in, proj_out, queries, store,
    new_grads, store_out, new_out,
    acts_v, outg_v, pin_v, pout_v, raw, turned, own, score_rows, work, order_m, lent, borrowed,
    pieces, plane_slots, column_slots, totals,
    load_sems, gs, gr, fs, fr, ps, pr, cs, cr, ts, tr,
):
    g = lax.axis_index("grp")
    f = lax.axis_index("fsdp")
    n_docs, length, features = acts.shape
    rank = proj_in.shape[0]
    here, width = queries.shape
    stored = store.shape[0]
    n_chips = n_fsdp // 2
    chip = f // 2
    core = lax.rem(f, 2)
    cut = here // PIECE
    share = rank // n_fsdp
    pitch = rank + 8
    spare = score_rows.shape[1] - stored
    mine = n_chips * here
    y = chip // 2
    x = lax.rem(chip, 2)
    per_unit = UNIT // here // 2
    n_units = n_chips // (UNIT // here)
    my_unit = y // per_unit
    my_place = lax.rem(y, per_unit)
    mesh_id = pl.DeviceIdType.MESH

    def in_plane(d):
        return {"grp": g, "fsdp": lax.rem(f + d, n_fsdp)}

    def in_column(d):
        return {"grp": lax.rem(g + d, n_grp), "fsdp": f}

    def rows_of(index, p):
        return raw.at[pl.ds(pl.multiple_of(index * here + p * PIECE, PIECE), PIECE)]

    def at(step, p, cross):
        return ((step[0] * per_unit + step[1]) * 2 + cross) * cut + p

    def moved(step, sign):
        unit = lax.rem(my_unit + n_units + sign * step[0], n_units)
        return unit * per_unit + lax.rem(my_place + per_unit + sign * step[1], per_unit)

    def block_copy(kind, step, p):
        across = (y * 2 + 1 - x) * 2 + core
        onward = (moved(step, 1) * 2 + x) * 2 + core
        if kind == "cross":
            source, target, where = chip, across, at((0, 0), p, 1)
        elif kind == "along":
            source, target, where = chip, onward, at(step, p, 0)
        elif p < cut // 2:
            source, target, where = y * 2 + 1 - x, onward, at(step, p, 1)
        else:
            source, target, where = moved(step, -1) * 2 + x, across, at(step, p, 1)
        rows = rows_of(source, p)
        return pltpu.make_async_remote_copy(
            src_ref=rows if kind == "relay" else queries.at[pl.ds(p * PIECE, PIECE)], dst_ref=rows_of(source, p),
            send_sem=gs.at[where], recv_sem=gr.at[where],
            device_id={"grp": g, "fsdp": target}, device_id_type=mesh_id)

    sibling = {"grp": g, "fsdp": f + 1 - 2 * core}

    def pass_copy(k):
        ends = (
            (store, score_rows.at[1, pl.ds(0, stored)]),
            (score_rows.at[0, pl.ds(stored, spare)], score_rows.at[1, pl.ds(stored, spare)]),
        ) + tuple((lent.at[e], borrowed.at[e]) for e in range(n_units))
        return pltpu.make_async_remote_copy(
            src_ref=ends[k][0], dst_ref=ends[k][1], send_sem=fs.at[k], recv_sem=fr.at[k],
            device_id=sibling, device_id_type=mesh_id)

    own_rows = raw.at[pl.ds(pl.multiple_of(chip * here, here), here)]
    loads = [
        pltpu.make_async_copy(src, dst, load_sems.at[i])
        for i, (src, dst) in enumerate((
            (acts, acts_v), (proj_in, pin_v), (out_grads, outg_v), (proj_out, pout_v),
            (queries, own_rows), (store, score_rows.at[0, pl.ds(0, stored)])))
    ]
    for load in loads:
        load.start()

    barrier = pltpu.get_barrier_semaphore()

    def greet_plane(d, _):
        pl.semaphore_signal(barrier, inc=1, device_id=in_plane(d), device_id_type=mesh_id)
        return 0

    def greet_column(d, _):
        pl.semaphore_signal(barrier, inc=1, device_id=in_column(d), device_id_type=mesh_id)
        return 0

    lax.fori_loop(1, n_fsdp, greet_plane, 0)
    lax.fori_loop(1, n_grp, greet_column, 0)

    order = send_order(n_units, per_unit, cut)
    marks = [0] + [len(order) * m // 12 for m in MARKS] + [len(order)]
    landed = set()

    def land(kind, step, p):
        if (kind, step, p) not in landed:
            landed.add((kind, step, p))
            block_copy(kind, step, p).wait_recv()

    def send_part(j):
        for kind, step, p in order[marks[j] : marks[j + 1]]:
            if kind == "relay":
                if p < cut // 2:
                    land("cross", (0, 0), p)
                else:
                    land("along", step, p)
            block_copy(kind, step, p).start()

    for load in loads[:4]:
        load.wait()

    tokens = lax.broadcasted_iota(jnp.int32, (length, 2 * rank), 0)
    lanes = lax.broadcasted_iota(jnp.int32, (rank, 2 * rank), 1)
    rows = lax.broadcasted_iota(jnp.int32, (rank, 2 * rank), 0)
    total = jnp.zeros((2 * rank, 2 * rank), F32)
    count = 0
    per_doc = []
    for doc in range(n_docs):
        in_proj = lax.dot_general(acts_v[doc], pin_v[...], NT, preferred_element_type=F32)
        out_proj = lax.dot_general(outg_v[doc], pout_v[...], NT, preferred_element_type=F32)
        both = jnp.concatenate([in_proj, out_proj], axis=1)
        size = lengths[doc]
        both = jnp.where(tokens < size, both, 0.0)
        gram = lax.dot_general(both, both, TN, precision=HIGHEST, preferred_element_type=F32)
        total = total + gram
        count = count + jnp.minimum(size, length)
        per_doc.append(gram[rank:, :rank] / size.astype(F32))
    packed = jnp.where(lanes < rank, total[:rank, :], total[rank:, :])
    counts = jnp.zeros((8, 2 * rank), F32) + count.astype(F32)
    for i in range(n_fsdp):
        piece = packed[i * share : (i + 1) * share, :]
        if share < 8:
            piece = jnp.concatenate([piece, jnp.zeros((8 - share, 2 * rank), F32)], axis=0)
        pieces[i, : piece.shape[0], :] = piece
        pieces[i, piece.shape[0] :, :] = counts

    def scatter_copy(d):
        return pltpu.make_async_remote_copy(
            src_ref=pieces.at[lax.rem(f + d, n_fsdp)], dst_ref=plane_slots.at[f],
            send_sem=ps.at[d], recv_sem=pr.at[d], device_id=in_plane(d), device_id_type=mesh_id)

    def column_copy(d):
        return pltpu.make_async_remote_copy(
            src_ref=column_slots.at[g], dst_ref=column_slots.at[g],
            send_sem=cs.at[d], recv_sem=cr.at[d], device_id=in_column(d), device_id_type=mesh_id)

    def total_copy(d):
        return pltpu.make_async_remote_copy(
            src_ref=totals.at[f], dst_ref=totals.at[f],
            send_sem=ts.at[d], recv_sem=tr.at[d], device_id=in_plane(d), device_id_type=mesh_id)

    block = 4 * rank
    eye = jnp.where(
        lax.broadcasted_iota(jnp.int32, (block, block), 0) == lax.broadcasted_iota(jnp.int32, (block, block), 1),
        1.0, 0.0).astype(BF16)

    def turn(e):
        unit = lax.rem(my_unit + n_units - e, n_units)
        unit_rows = pl.ds(pl.multiple_of(unit * UNIT, UNIT), UNIT)
        for i in range(width // block):
            chunk = raw[unit_rows, i * block : (i + 1) * block]
            part = lax.dot_general(eye, chunk, NT, preferred_element_type=F32)
            for a in range(4):
                start = (4 * i + a) * pitch
                work[0, start : start + rank, :] = part[a * rank : (a + 1) * rank, :]
        for b in range(rank):
            turned[e, b * rank : (b + 1) * rank, :] = work[0, pl.ds(b, rank, stride=pitch), :].astype(BF16)

    def arrive(e):
        for kind, step, p in order:
            if step[0] == e:
                land(kind, step, p)

    pl.semaphore_wait(barrier, n_fsdp - 1 + n_grp - 1)
    for d in range(1, n_fsdp):
        scatter_copy(d).start()
    send_part(0)
    pass_copy(0).start()
    plane_slots[f] = pieces[f]
    flat = [
        jnp.concatenate([grad[a : a + 1, :] for a in range(rank)], axis=1) for grad in per_doc
    ]
    fresh = jnp.concatenate(
        flat + [jnp.zeros((spare - n_docs, width), F32)], axis=0).astype(BF16)
    score_rows[0, stored:, :] = fresh
    pass_copy(1).start()
    new_grads[...] = fresh[:n_docs]
    for d in range(1, n_fsdp):
        scatter_copy(d).wait()
    summed = plane_slots[0]
    for i in range(1, n_fsdp):
        summed = summed + plane_slots[i]
    column_slots[g] = summed
    for d in range(1, n_grp):
        column_copy(d).start()
    send_part(1)
    for d in range(1, n_grp):
        column_copy(d).wait()
    summed = column_slots[0]
    for i in range(1, n_grp):
        summed = summed + column_slots[i]
    totals[f] = summed
    for d in range(1, n_fsdp):
        total_copy(d).start()
    send_part(2)
    wide_row = lax.broadcasted_iota(jnp.int32, order_m.shape, 0)
    wide_lane = lax.broadcasted_iota(jnp.int32, order_m.shape, 1)
    from_core = lax.rem(wide_lane // here, 2)
    from_unit = lax.rem(my_unit + n_units - wide_lane // (2 * UNIT), n_units)
    from_row = (
        jnp.where(from_core == core, 0, mine) + from_unit * UNIT
        + lax.rem(wide_lane // (2 * here), UNIT // here) * here + lax.rem(wide_lane, here))
    order_m[...] = jnp.where(wide_row == from_row, 1.0, 0.0).astype(BF16)

    loads[4].wait()
    loads[5].wait()
    arrive(0)
    turn(0)
    for d in range(1, n_fsdp):
        total_copy(d).wait()

    covariance = jnp.concatenate([totals[i, :share, :] for i in range(n_fsdp)], axis=0)
    covariance = covariance / summed[summed.shape[0] - 1 :, :]
    diagonal = (rows == lanes) | (rows + rank == lanes)
    on_diagonal = jnp.where(diagonal, covariance, 0.0)
    in_trace = jnp.sum(jnp.where(lanes < rank, on_diagonal, 0.0))
    out_trace = jnp.sum(jnp.where(lanes < rank, 0.0, on_diagonal))
    ridge = jnp.where(lanes < rank, 0.1 * in_trace / rank, 0.1 * out_trace / rank)
    both = invert_pair(covariance + jnp.where(diagonal, ridge, 0.0), rank)

    ih, im, il = split3(both[:, :rank])
    zero = jnp.zeros((rank, rank), BF16)
    in_left = jnp.concatenate([
        jnp.concatenate([ih, ih, ih], axis=1),
        jnp.concatenate([im, im, zero], axis=1),
        jnp.concatenate([il, zero, zero], axis=1)], axis=0)
    out_left = jnp.concatenate(split3(both[:, rank:]), axis=0)

    pass_copy(0).wait()
    pass_copy(1).wait()
    own_scores = []
    for e in range(n_units):
        if e:
            arrive(e)
            turn(e)
        for b in range(0, rank, 2):
            right = jnp.concatenate([turned[e, (b + j) * rank : (b + j + 1) * rank, :] for j in range(2)], axis=1)
            part = jnp.dot(out_left, right, preferred_element_type=F32)
            part = part[:rank] + (part[rank : 2 * rank] + part[2 * rank :])
            for j in range(2):
                work[e, pl.ds(b + j, rank, stride=pitch), :] = part[:, j * UNIT : (j + 1) * UNIT]
        for a in range(0, rank, 2):
            half_done = jnp.concatenate(
                [work[e, (a + j) * pitch : (a + j) * pitch + rank, :] for j in range(2)], axis=1)
            right = jnp.concatenate(split3(half_done), axis=0)
            part = jnp.dot(in_left, right, preferred_element_type=F32)
            part = part[:rank] + (part[rank : 2 * rank] + part[2 * rank :])
            for j in range(2):
                own[e, (a + j) * rank : (a + j + 1) * rank, :] = part[:, j * UNIT : (j + 1) * UNIT].astype(BF16)
        lent[e] = jnp.dot(score_rows[1], own[e], preferred_element_type=F32).astype(BF16)
        pass_copy(2 + e).start()
        own_scores.append(jnp.dot(score_rows[0], own[e], preferred_element_type=F32).astype(BF16))
    for e in range(n_units):
        pass_copy(2 + e).wait()
    scores = jnp.concatenate(own_scores + [borrowed[e] for e in range(n_units)], axis=1)
    scores = jnp.dot(scores, order_m[...], preferred_element_type=F32).astype(BF16)
    for kind, step, p in order:
        block_copy(kind, step, p).wait_send()
    store_out[...] = scores[:stored]
    new_out[...] = scores[stored : stored + n_docs]


PIECE = 16
UNIT = 128
AHEAD = 8
MARKS = (4, 8)


def hand_over(*refs):
    for source, target in zip(refs[:3], refs[3:]):
        target[...] = source[...]


def influence(n_grp, n_fsdp, doc_lengths, acts, out_grads, proj_in, proj_out, queries, store):
    n_docs = acts.shape[0]
    rank = proj_in.shape[0]
    here, width = queries.shape
    stored = store.shape[0]
    n_queries = n_fsdp * here
    dma = pltpu.SemaphoreType.DMA
    slot = (-(-(rank // n_fsdp) // 8) * 8 + 8, 2 * rank)
    score_rows = -(-(stored + n_docs) // 16) * 16
    copies = dma((n_fsdp // 2 * (here // PIECE),))
    mine = n_queries // 2
    results = pl.pallas_call(
        functools.partial(influence_kernel, n_grp, n_fsdp),
        out_shape=(
            VMEM((n_docs, width), BF16),
            VMEM((stored, n_queries), BF16),
            VMEM((n_docs, n_queries), BF16),
        ),
        in_specs=[pl.BlockSpec(memory_space=pltpu.SMEM)] + [pl.BlockSpec(memory_space=ANY)] * 6,
        out_specs=tuple([pl.BlockSpec(memory_space=VMEM)] * 3),
        scratch_shapes=[
            VMEM(acts.shape, BF16), VMEM(out_grads.shape, BF16),
            VMEM(proj_in.shape, BF16), VMEM(proj_out.shape, BF16),
            VMEM((mine, width), BF16), VMEM((mine // UNIT, width, UNIT), BF16),
            VMEM((mine // UNIT, width, UNIT), BF16), VMEM((2, score_rows, width), BF16),
            VMEM((mine // UNIT, rank * (rank + 8), UNIT), F32),
            VMEM((n_queries, n_queries), BF16),
            VMEM((mine // UNIT, score_rows, UNIT), BF16), VMEM((mine // UNIT, score_rows, UNIT), BF16),
            VMEM((n_fsdp,) + slot, F32), VMEM((n_fsdp,) + slot, F32),
            VMEM((n_grp,) + slot, F32), VMEM((n_fsdp,) + slot, F32),
            dma((6,)), copies, copies, dma((2 + mine // UNIT,)), dma((2 + mine // UNIT,)),
            dma((n_fsdp,)), dma((n_fsdp,)), dma((n_grp,)), dma((n_grp,)), dma((n_fsdp,)), dma((n_fsdp,)),
        ],
        compiler_params=pltpu.CompilerParams(
            collective_id=0, has_side_effects=True, vmem_limit_bytes=56 * 2**20),
    )(doc_lengths, acts, out_grads, proj_in, proj_out, queries, store)
    return pl.pallas_call(
        hand_over,
        out_shape=tuple(jax.ShapeDtypeStruct(r.shape, r.dtype) for r in results),
        in_specs=[pl.BlockSpec(memory_space=VMEM)] * 3,
        out_specs=tuple([pl.BlockSpec(memory_space=VMEM)] * 3),
        compiler_params=pltpu.CompilerParams(vmem_limit_bytes=4 * 2**20),
    )(*results)


def solution(mesh):
    n_grp, n_fsdp = mesh.shape["grp"], mesh.shape["fsdp"]

    def shards(acts, out_grads, doc_lengths, proj_in, proj_out, store_grads, queries):
        return influence(
            n_grp, n_fsdp, doc_lengths, acts, out_grads, proj_in, proj_out, queries, store_grads)

    rows = P(("grp", "fsdp"), None)
    placed = (
        P(("grp", "fsdp"), None, None),
        P(("grp", "fsdp"), None, None),
        P(("grp", "fsdp")),
        P(),
        P(),
        rows,
        P("fsdp", None),
    )
    return jax.shard_map(
        shards, mesh=mesh, in_specs=placed, out_specs=(rows, rows, rows), check_vma=False)
```

```python
import functools

import jax
import jax.numpy as jnp
from jax import lax
from jax.experimental import pallas as pl
from jax.experimental.pallas import tpu as pltpu
from jax.sharding import PartitionSpec as P

F32 = jnp.float32
BF16 = jnp.bfloat16
ANY = pl.ANY
VMEM = pltpu.VMEM
HIGHEST = lax.Precision.HIGHEST
NT = (((1,), (1,)), ((), ()))
TN = (((0,), (0,)), ((), ()))


def invert_pair(matrix, rank):
    lanes = lax.broadcasted_iota(jnp.int32, (8, 2 * rank), 1)
    subs = lax.broadcasted_iota(jnp.int32, (8, 2 * rank), 0)
    left = lanes < rank
    local = jnp.where(left, lanes, lanes - rank)
    blocks = [matrix[i : i + 8, :] for i in range(0, rank, 8)]
    for first in range(0, rank, AHEAD):
        ahead = range(first, first + AHEAD)
        columns = [
            [jnp.take_along_axis(block, jnp.where(left, k, rank + k), axis=1) for block in blocks]
            for k in ahead
        ]
        for k in ahead:
            at, row = k // 8, k % 8
            column = columns[k - first]
            inverse_pivot = 1.0 / column[at][row : row + 1, :]
            at_pivot = local == k
            scaled = jnp.where(at_pivot[:1], 1.0, blocks[at][row : row + 1, :]) * inverse_pivot
            for later in range(k + 1 - first, AHEAD):
                part = columns[later][at][row : row + 1, :] * inverse_pivot
                reduced = [c - d * part for c, d in zip(columns[later], column)]
                reduced[at] = jnp.where(subs == row, part, reduced[at])
                columns[later] = reduced
            reduced = [jnp.where(at_pivot, 0.0, c) - d * scaled for c, d in zip(blocks, column)]
            reduced[at] = jnp.where(subs == row, scaled, reduced[at])
            blocks = reduced
    return jnp.concatenate(blocks, axis=0)


def split3(value):
    high = value.astype(BF16)
    rest = value - high.astype(F32)
    middle = rest.astype(BF16)
    low = (rest - middle.astype(F32)).astype(BF16)
    return high, middle, low


def send_order(n_units, per_unit, cut):
    steps = [(e, i) for e in range(n_units) for i in range(per_unit)][1:]
    order = []
    for p in range(cut):
        order.append(("cross", (0, 0), p))
        order.extend(("along", step, (p + cut // 2) % cut) for step in steps)
    for p in range(max(cut // 2, cut - cut // 2)):
        for step in steps:
            order.extend(("relay", step, q) for q in (p, cut // 2 + p) if p < cut // 2 or q == cut // 2 + p)
    return order


def influence_kernel(
    n_grp, n_fsdp,
    lengths, acts, out_grads, proj_in, proj_out, queries, store,
    new_grads, store_out, new_out,
    acts_v, outg_v, pin_v, pout_v, raw, turned, own, score_rows, work, order_m, lent, borrowed,
    pieces, plane_slots, column_slots, totals,
    load_sems, gs, gr, fs, fr, ps, pr, cs, cr, ts, tr,
):
    g = lax.axis_index("grp")
    f = lax.axis_index("fsdp")
    n_docs, length, features = acts.shape
    rank = proj_in.shape[0]
    here, width = queries.shape
    stored = store.shape[0]
    n_chips = n_fsdp // 2
    chip = f // 2
    core = lax.rem(f, 2)
    cut = here // PIECE
    share = rank // n_fsdp
    pitch = rank + 8
    spare = score_rows.shape[1] - stored
    mine = n_chips * here
    y = chip // 2
    x = lax.rem(chip, 2)
    per_unit = UNIT // here // 2
    n_units = n_chips // (UNIT // here)
    my_unit = y // per_unit
    my_place = lax.rem(y, per_unit)
    mesh_id = pl.DeviceIdType.MESH

    def in_plane(d):
        return {"grp": g, "fsdp": lax.rem(f + d, n_fsdp)}

    def in_column(d):
        return {"grp": lax.rem(g + d, n_grp), "fsdp": f}

    def rows_of(index, p):
        return raw.at[pl.ds(pl.multiple_of(index * here + p * PIECE, PIECE), PIECE)]

    def at(step, p, cross):
        return ((step[0] * per_unit + step[1]) * 2 + cross) * cut + p

    def moved(step, sign):
        unit = lax.rem(my_unit + n_units + sign * step[0], n_units)
        return unit * per_unit + lax.rem(my_place + per_unit + sign * step[1], per_unit)

    def block_copy(kind, step, p):
        across = (y * 2 + 1 - x) * 2 + core
        onward = (moved(step, 1) * 2 + x) * 2 + core
        if kind == "cross":
            source, target, where = chip, across, at((0, 0), p, 1)
        elif kind == "along":
            source, target, where = chip, onward, at(step, p, 0)
        elif p < cut // 2:
            source, target, where = y * 2 + 1 - x, onward, at(step, p, 1)
        else:
            source, target, where = moved(step, -1) * 2 + x, across, at(step, p, 1)
        rows = rows_of(source, p)
        return pltpu.make_async_remote_copy(
            src_ref=rows if kind == "relay" else queries.at[pl.ds(p * PIECE, PIECE)], dst_ref=rows_of(source, p),
            send_sem=gs.at[where], recv_sem=gr.at[where],
            device_id={"grp": g, "fsdp": target}, device_id_type=mesh_id)

    sibling = {"grp": g, "fsdp": f + 1 - 2 * core}

    def pass_copy(k):
        ends = (
            (store, score_rows.at[1, pl.ds(0, stored)]),
            (score_rows.at[0, pl.ds(stored, spare)], score_rows.at[1, pl.ds(stored, spare)]),
        ) + tuple((lent.at[e], borrowed.at[e]) for e in range(n_units))
        return pltpu.make_async_remote_copy(
            src_ref=ends[k][0], dst_ref=ends[k][1], send_sem=fs.at[k], recv_sem=fr.at[k],
            device_id=sibling, device_id_type=mesh_id)

    own_rows = raw.at[pl.ds(pl.multiple_of(chip * here, here), here)]
    loads = [
        pltpu.make_async_copy(src, dst, load_sems.at[i])
        for i, (src, dst) in enumerate((
            (acts, acts_v), (proj_in, pin_v), (out_grads, outg_v), (proj_out, pout_v),
            (queries, own_rows), (store, score_rows.at[0, pl.ds(0, stored)])))
    ]
    for load in loads:
        load.start()

    barrier = pltpu.get_barrier_semaphore()

    def greet_plane(d, _):
        pl.semaphore_signal(barrier, inc=1, device_id=in_plane(d), device_id_type=mesh_id)
        return 0

    def greet_column(d, _):
        pl.semaphore_signal(barrier, inc=1, device_id=in_column(d), device_id_type=mesh_id)
        return 0

    lax.fori_loop(1, n_fsdp, greet_plane, 0)
    lax.fori_loop(1, n_grp, greet_column, 0)

    order = send_order(n_units, per_unit, cut)
    marks = [0] + [len(order) * m // 12 for m in MARKS] + [len(order)]
    landed = set()

    def land(kind, step, p):
        if (kind, step, p) not in landed:
            landed.add((kind, step, p))
            block_copy(kind, step, p).wait_recv()

    def send_part(j):
        for kind, step, p in order[marks[j] : marks[j + 1]]:
            if kind == "relay":
                if p < cut // 2:
                    land("cross", (0, 0), p)
                else:
                    land("along", step, p)
            block_copy(kind, step, p).start()

    for load in loads[:4]:
        load.wait()

    tokens = lax.broadcasted_iota(jnp.int32, (length, 2 * rank), 0)
    lanes = lax.broadcasted_iota(jnp.int32, (rank, 2 * rank), 1)
    rows = lax.broadcasted_iota(jnp.int32, (rank, 2 * rank), 0)
    total = jnp.zeros((2 * rank, 2 * rank), F32)
    count = 0
    per_doc = []
    for doc in range(n_docs):
        in_proj = lax.dot_general(acts_v[doc], pin_v[...], NT, preferred_element_type=F32)
        out_proj = lax.dot_general(outg_v[doc], pout_v[...], NT, preferred_element_type=F32)
        both = jnp.concatenate([in_proj, out_proj], axis=1)
        size = lengths[doc]
        both = jnp.where(tokens < size, both, 0.0)
        gram = lax.dot_general(both, both, TN, precision=HIGHEST, preferred_element_type=F32)
        total = total + gram
        count = count + jnp.minimum(size, length)
        per_doc.append(gram[rank:, :rank] / size.astype(F32))
    packed = jnp.where(lanes < rank, total[:rank, :], total[rank:, :])
    counts = jnp.zeros((8, 2 * rank), F32) + count.astype(F32)
    for i in range(n_fsdp):
        piece = packed[i * share : (i + 1) * share, :]
        if share < 8:
            piece = jnp.concatenate([piece, jnp.zeros((8 - share, 2 * rank), F32)], axis=0)
        pieces[i, : piece.shape[0], :] = piece
        pieces[i, piece.shape[0] :, :] = counts

    def scatter_copy(d):
        return pltpu.make_async_remote_copy(
            src_ref=pieces.at[lax.rem(f + d, n_fsdp)], dst_ref=plane_slots.at[f],
            send_sem=ps.at[d], recv_sem=pr.at[d], device_id=in_plane(d), device_id_type=mesh_id)

    def column_copy(d):
        return pltpu.make_async_remote_copy(
            src_ref=column_slots.at[g], dst_ref=column_slots.at[g],
            send_sem=cs.at[d], recv_sem=cr.at[d], device_id=in_column(d), device_id_type=mesh_id)

    def total_copy(d):
        return pltpu.make_async_remote_copy(
            src_ref=totals.at[f], dst_ref=totals.at[f],
            send_sem=ts.at[d], recv_sem=tr.at[d], device_id=in_plane(d), device_id_type=mesh_id)

    block = 4 * rank
    eye = jnp.where(
        lax.broadcasted_iota(jnp.int32, (block, block), 0) == lax.broadcasted_iota(jnp.int32, (block, block), 1),
        1.0, 0.0).astype(BF16)

    def turn(e):
        unit = lax.rem(my_unit + n_units - e, n_units)
        unit_rows = pl.ds(pl.multiple_of(unit * UNIT, UNIT), UNIT)
        for i in range(width // block):
            chunk = raw[unit_rows, i * block : (i + 1) * block]
            part = lax.dot_general(eye, chunk, NT, preferred_element_type=F32)
            for a in range(4):
                start = (4 * i + a) * pitch
                work[0, start : start + rank, :] = part[a * rank : (a + 1) * rank, :]
        for b in range(rank):
            turned[e, b * rank : (b + 1) * rank, :] = work[0, pl.ds(b, rank, stride=pitch), :].astype(BF16)

    def arrive(e):
        for kind, step, p in order:
            if step[0] == e:
                land(kind, step, p)

    pl.semaphore_wait(barrier, n_fsdp - 1 + n_grp - 1)
    for d in range(1, n_fsdp):
        scatter_copy(d).start()
    send_part(0)
    pass_copy(0).start()
    plane_slots[f] = pieces[f]
    flat = [
        jnp.concatenate([grad[a : a + 1, :] for a in range(rank)], axis=1) for grad in per_doc
    ]
    fresh = jnp.concatenate(
        flat + [jnp.zeros((spare - n_docs, width), F32)], axis=0).astype(BF16)
    score_rows[0, stored:, :] = fresh
    pass_copy(1).start()
    new_grads[...] = fresh[:n_docs]
    for d in range(1, n_fsdp):
        scatter_copy(d).wait()
    summed = plane_slots[0]
    for i in range(1, n_fsdp):
        summed = summed + plane_slots[i]
    column_slots[g] = summed
    for d in range(1, n_grp):
        column_copy(d).start()
    send_part(1)
    for d in range(1, n_grp):
        column_copy(d).wait()
    summed = column_slots[0]
    for i in range(1, n_grp):
        summed = summed + column_slots[i]
    totals[f] = summed
    for d in range(1, n_fsdp):
        total_copy(d).start()
    send_part(2)
    wide_row = lax.broadcasted_iota(jnp.int32, order_m.shape, 0)
    wide_lane = lax.broadcasted_iota(jnp.int32, order_m.shape, 1)
    from_core = lax.rem(wide_lane // here, 2)
    from_unit = lax.rem(my_unit + n_units - wide_lane // (2 * UNIT), n_units)
    from_row = (
        jnp.where(from_core == core, 0, mine) + from_unit * UNIT
        + lax.rem(wide_lane // (2 * here), UNIT // here) * here + lax.rem(wide_lane, here))
    order_m[...] = jnp.where(wide_row == from_row, 1.0, 0.0).astype(BF16)

    loads[4].wait()
    loads[5].wait()
    for d in range(1, n_fsdp):
        total_copy(d).wait()

    covariance = jnp.concatenate([totals[i, :share, :] for i in range(n_fsdp)], axis=0)
    covariance = covariance / summed[summed.shape[0] - 1 :, :]
    diagonal = (rows == lanes) | (rows + rank == lanes)
    on_diagonal = jnp.where(diagonal, covariance, 0.0)
    in_trace = jnp.sum(jnp.where(lanes < rank, on_diagonal, 0.0))
    out_trace = jnp.sum(jnp.where(lanes < rank, 0.0, on_diagonal))
    ridge = jnp.where(lanes < rank, 0.1 * in_trace / rank, 0.1 * out_trace / rank)
    both = invert_pair(covariance + jnp.where(diagonal, ridge, 0.0), rank)

    ih, im, il = split3(both[:, :rank])
    zero = jnp.zeros((rank, rank), BF16)
    in_left = jnp.concatenate([
        jnp.concatenate([ih, ih, ih], axis=1),
        jnp.concatenate([im, im, zero], axis=1),
        jnp.concatenate([il, zero, zero], axis=1)], axis=0)
    out_left = jnp.concatenate(split3(both[:, rank:]), axis=0)

    pass_copy(0).wait()
    pass_copy(1).wait()
    own_scores = []
    for e in range(n_units):
        arrive(e)
        turn(e)
        for b in range(0, rank, 2):
            right = jnp.concatenate([turned[e, (b + j) * rank : (b + j + 1) * rank, :] for j in range(2)], axis=1)
            part = jnp.dot(out_left, right, preferred_element_type=F32)
            part = part[:rank] + (part[rank : 2 * rank] + part[2 * rank :])
            for j in range(2):
                work[e, pl.ds(b + j, rank, stride=pitch), :] = part[:, j * UNIT : (j + 1) * UNIT]
        for a in range(0, rank, 2):
            half_done = jnp.concatenate(
                [work[e, (a + j) * pitch : (a + j) * pitch + rank, :] for j in range(2)], axis=1)
            right = jnp.concatenate(split3(half_done), axis=0)
            part = jnp.dot(in_left, right, preferred_element_type=F32)
            part = part[:rank] + (part[rank : 2 * rank] + part[2 * rank :])
            for j in range(2):
                own[e, (a + j) * rank : (a + j + 1) * rank, :] = part[:, j * UNIT : (j + 1) * UNIT].astype(BF16)
        lent[e] = jnp.dot(score_rows[1], own[e], preferred_element_type=F32).astype(BF16)
        pass_copy(2 + e).start()
        own_scores.append(jnp.dot(score_rows[0], own[e], preferred_element_type=F32).astype(BF16))
    for e in range(n_units):
        pass_copy(2 + e).wait()
    scores = jnp.concatenate(own_scores + [borrowed[e] for e in range(n_units)], axis=1)
    scores = jnp.dot(scores, order_m[...], preferred_element_type=F32).astype(BF16)
    for kind, step, p in order:
        block_copy(kind, step, p).wait_send()
    store_out[...] = scores[:stored]
    new_out[...] = scores[stored : stored + n_docs]


PIECE = 16
UNIT = 128
AHEAD = 8
MARKS = (4, 6)


def hand_over(*refs):
    for source, target in zip(refs[:3], refs[3:]):
        target[...] = source[...]


def influence(n_grp, n_fsdp, doc_lengths, acts, out_grads, proj_in, proj_out, queries, store):
    n_docs = acts.shape[0]
    rank = proj_in.shape[0]
    here, width = queries.shape
    stored = store.shape[0]
    n_queries = n_fsdp * here
    dma = pltpu.SemaphoreType.DMA
    slot = (-(-(rank // n_fsdp) // 8) * 8 + 8, 2 * rank)
    score_rows = -(-(stored + n_docs) // 16) * 16
    copies = dma((n_fsdp // 2 * (here // PIECE),))
    mine = n_queries // 2
    results = pl.pallas_call(
        functools.partial(influence_kernel, n_grp, n_fsdp),
        out_shape=(
            VMEM((n_docs, width), BF16),
            VMEM((stored, n_queries), BF16),
            VMEM((n_docs, n_queries), BF16),
        ),
        in_specs=[pl.BlockSpec(memory_space=pltpu.SMEM)] + [pl.BlockSpec(memory_space=ANY)] * 6,
        out_specs=tuple([pl.BlockSpec(memory_space=VMEM)] * 3),
        scratch_shapes=[
            VMEM(acts.shape, BF16), VMEM(out_grads.shape, BF16),
            VMEM(proj_in.shape, BF16), VMEM(proj_out.shape, BF16),
            VMEM((mine, width), BF16), VMEM((mine // UNIT, width, UNIT), BF16),
            VMEM((mine // UNIT, width, UNIT), BF16), VMEM((2, score_rows, width), BF16),
            VMEM((mine // UNIT, rank * (rank + 8), UNIT), F32),
            VMEM((n_queries, n_queries), BF16),
            VMEM((mine // UNIT, score_rows, UNIT), BF16), VMEM((mine // UNIT, score_rows, UNIT), BF16),
            VMEM((n_fsdp,) + slot, F32), VMEM((n_fsdp,) + slot, F32),
            VMEM((n_grp,) + slot, F32), VMEM((n_fsdp,) + slot, F32),
            dma((6,)), copies, copies, dma((2 + mine // UNIT,)), dma((2 + mine // UNIT,)),
            dma((n_fsdp,)), dma((n_fsdp,)), dma((n_grp,)), dma((n_grp,)), dma((n_fsdp,)), dma((n_fsdp,)),
        ],
        compiler_params=pltpu.CompilerParams(
            collective_id=0, has_side_effects=True, vmem_limit_bytes=56 * 2**20),
    )(doc_lengths, acts, out_grads, proj_in, proj_out, queries, store)
    return pl.pallas_call(
        hand_over,
        out_shape=tuple(jax.ShapeDtypeStruct(r.shape, r.dtype) for r in results),
        in_specs=[pl.BlockSpec(memory_space=VMEM)] * 3,
        out_specs=tuple([pl.BlockSpec(memory_space=VMEM)] * 3),
        compiler_params=pltpu.CompilerParams(vmem_limit_bytes=4 * 2**20),
    )(*results)


def solution(mesh):
    n_grp, n_fsdp = mesh.shape["grp"], mesh.shape["fsdp"]

    def shards(acts, out_grads, doc_lengths, proj_in, proj_out, store_grads, queries):
        return influence(
            n_grp, n_fsdp, doc_lengths, acts, out_grads, proj_in, proj_out, queries, store_grads)

    rows = P(("grp", "fsdp"), None)
    placed = (
        P(("grp", "fsdp"), None, None),
        P(("grp", "fsdp"), None, None),
        P(("grp", "fsdp")),
        P(),
        P(),
        rows,
        P("fsdp", None),
    )
    return jax.shard_map(
        shards, mesh=mesh, in_specs=placed, out_specs=(rows, rows, rows), check_vma=False)
```

```python
import functools

import jax
import jax.numpy as jnp
from jax import lax
from jax.experimental import pallas as pl
from jax.experimental.pallas import tpu as pltpu
from jax.sharding import PartitionSpec as P

F32 = jnp.float32
BF16 = jnp.bfloat16
ANY = pl.ANY
VMEM = pltpu.VMEM
HIGHEST = lax.Precision.HIGHEST
NT = (((1,), (1,)), ((), ()))
TN = (((0,), (0,)), ((), ()))


def invert_pair(matrix, rank):
    lanes = lax.broadcasted_iota(jnp.int32, (8, 2 * rank), 1)
    subs = lax.broadcasted_iota(jnp.int32, (8, 2 * rank), 0)
    left = lanes < rank
    local = jnp.where(left, lanes, lanes - rank)
    blocks = [matrix[i : i + 8, :] for i in range(0, rank, 8)]
    for first in range(0, rank, AHEAD):
        ahead = range(first, first + AHEAD)
        columns = [
            [jnp.take_along_axis(block, jnp.where(left, k, rank + k), axis=1) for block in blocks]
            for k in ahead
        ]
        for k in ahead:
            at, row = k // 8, k % 8
            column = columns[k - first]
            inverse_pivot = 1.0 / column[at][row : row + 1, :]
            at_pivot = local == k
            scaled = jnp.where(at_pivot[:1], 1.0, blocks[at][row : row + 1, :]) * inverse_pivot
            for later in range(k + 1 - first, AHEAD):
                part = columns[later][at][row : row + 1, :] * inverse_pivot
                reduced = [c - d * part for c, d in zip(columns[later], column)]
                reduced[at] = jnp.where(subs == row, part, reduced[at])
                columns[later] = reduced
            reduced = [jnp.where(at_pivot, 0.0, c) - d * scaled for c, d in zip(blocks, column)]
            reduced[at] = jnp.where(subs == row, scaled, reduced[at])
            blocks = reduced
    return jnp.concatenate(blocks, axis=0)


def split3(value):
    high = value.astype(BF16)
    rest = value - high.astype(F32)
    middle = rest.astype(BF16)
    low = (rest - middle.astype(F32)).astype(BF16)
    return high, middle, low


def send_order(n_units, per_unit, cut):
    steps = [(e, i) for e in range(n_units) for i in range(per_unit)][1:]
    order = []
    for p in range(cut):
        order.append(("cross", (0, 0), p))
        order.extend(("along", step, (p + cut // 2) % cut) for step in steps)
    for p in range(max(cut // 2, cut - cut // 2)):
        for step in steps:
            order.extend(("relay", step, q) for q in (p, cut // 2 + p) if p < cut // 2 or q == cut // 2 + p)
    return order


def influence_kernel(
    n_grp, n_fsdp,
    lengths, acts, out_grads, proj_in, proj_out, queries, store,
    new_grads, store_out, new_out,
    acts_v, outg_v, pin_v, pout_v, raw, turned, own, score_rows, work, order_m, lent, borrowed,
    pieces, plane_slots, column_slots, totals,
    load_sems, gs, gr, fs, fr, ps, pr, cs, cr, ts, tr,
):
    g = lax.axis_index("grp")
    f = lax.axis_index("fsdp")
    n_docs, length, features = acts.shape
    rank = proj_in.shape[0]
    here, width = queries.shape
    stored = store.shape[0]
    n_chips = n_fsdp // 2
    chip = f // 2
    core = lax.rem(f, 2)
    cut = here // PIECE
    share = rank // n_fsdp
    pitch = rank + 8
    spare = score_rows.shape[1] - stored
    mine = n_chips * here
    y = chip // 2
    x = lax.rem(chip, 2)
    per_unit = UNIT // here // 2
    n_units = n_chips // (UNIT // here)
    my_unit = y // per_unit
    my_place = lax.rem(y, per_unit)
    mesh_id = pl.DeviceIdType.MESH

    def in_plane(d):
        return {"grp": g, "fsdp": lax.rem(f + d, n_fsdp)}

    def in_column(d):
        return {"grp": lax.rem(g + d, n_grp), "fsdp": f}

    def rows_of(index, p):
        return raw.at[pl.ds(pl.multiple_of(index * here + p * PIECE, PIECE), PIECE)]

    def at(step, p, cross):
        return ((step[0] * per_unit + step[1]) * 2 + cross) * cut + p

    def moved(step, sign):
        unit = lax.rem(my_unit + n_units + sign * step[0], n_units)
        return unit * per_unit + lax.rem(my_place + per_unit + sign * step[1], per_unit)

    def block_copy(kind, step, p):
        across = (y * 2 + 1 - x) * 2 + core
        onward = (moved(step, 1) * 2 + x) * 2 + core
        if kind == "cross":
            source, target, where = chip, across, at((0, 0), p, 1)
        elif kind == "along":
            source, target, where = chip, onward, at(step, p, 0)
        elif p < cut // 2:
            source, target, where = y * 2 + 1 - x, onward, at(step, p, 1)
        else:
            source, target, where = moved(step, -1) * 2 + x, across, at(step, p, 1)
        rows = rows_of(source, p)
        return pltpu.make_async_remote_copy(
            src_ref=rows if kind == "relay" else queries.at[pl.ds(p * PIECE, PIECE)], dst_ref=rows_of(source, p),
            send_sem=gs.at[where], recv_sem=gr.at[where],
            device_id={"grp": g, "fsdp": target}, device_id_type=mesh_id)

    sibling = {"grp": g, "fsdp": f + 1 - 2 * core}

    def pass_copy(k):
        ends = (
            (store, score_rows.at[1, pl.ds(0, stored)]),
            (score_rows.at[0, pl.ds(stored, spare)], score_rows.at[1, pl.ds(stored, spare)]),
        ) + tuple((lent.at[e], borrowed.at[e]) for e in range(n_units))
        return pltpu.make_async_remote_copy(
            src_ref=ends[k][0], dst_ref=ends[k][1], send_sem=fs.at[k], recv_sem=fr.at[k],
            device_id=sibling, device_id_type=mesh_id)

    own_rows = raw.at[pl.ds(pl.multiple_of(chip * here, here), here)]
    loads = [
        pltpu.make_async_copy(src, dst, load_sems.at[i])
        for i, (src, dst) in enumerate((
            (acts, acts_v), (proj_in, pin_v), (out_grads, outg_v), (proj_out, pout_v),
            (queries, own_rows), (store, score_rows.at[0, pl.ds(0, stored)])))
    ]
    for load in loads:
        load.start()

    barrier = pltpu.get_barrier_semaphore()

    def greet_plane(d, _):
        pl.semaphore_signal(barrier, inc=1, device_id=in_plane(d), device_id_type=mesh_id)
        return 0

    def greet_column(d, _):
        pl.semaphore_signal(barrier, inc=1, device_id=in_column(d), device_id_type=mesh_id)
        return 0

    lax.fori_loop(1, n_fsdp, greet_plane, 0)
    lax.fori_loop(1, n_grp, greet_column, 0)

    order = send_order(n_units, per_unit, cut)
    marks = [0] + [len(order) * m // 12 for m in MARKS] + [len(order)]
    landed = set()

    def land(kind, step, p):
        if (kind, step, p) not in landed:
            landed.add((kind, step, p))
            block_copy(kind, step, p).wait_recv()

    def send_part(j):
        for kind, step, p in order[marks[j] : marks[j + 1]]:
            if kind == "relay":
                if p < cut // 2:
                    land("cross", (0, 0), p)
                else:
                    land("along", step, p)
            block_copy(kind, step, p).start()

    for load in loads[:4]:
        load.wait()

    tokens = lax.broadcasted_iota(jnp.int32, (length, 2 * rank), 0)
    lanes = lax.broadcasted_iota(jnp.int32, (rank, 2 * rank), 1)
    rows = lax.broadcasted_iota(jnp.int32, (rank, 2 * rank), 0)
    total = jnp.zeros((2 * rank, 2 * rank), F32)
    count = 0
    per_doc = []
    for doc in range(n_docs):
        in_proj = lax.dot_general(acts_v[doc], pin_v[...], NT, preferred_element_type=F32)
        out_proj = lax.dot_general(outg_v[doc], pout_v[...], NT, preferred_element_type=F32)
        both = jnp.concatenate([in_proj, out_proj], axis=1)
        size = lengths[doc]
        both = jnp.where(tokens < size, both, 0.0)
        gram = lax.dot_general(both, both, TN, precision=HIGHEST, preferred_element_type=F32)
        total = total + gram
        count = count + jnp.minimum(size, length)
        per_doc.append(gram[rank:, :rank] / size.astype(F32))
    packed = jnp.where(lanes < rank, total[:rank, :], total[rank:, :])
    counts = jnp.zeros((8, 2 * rank), F32) + count.astype(F32)
    for i in range(n_fsdp):
        piece = packed[i * share : (i + 1) * share, :]
        if share < 8:
            piece = jnp.concatenate([piece, jnp.zeros((8 - share, 2 * rank), F32)], axis=0)
        pieces[i, : piece.shape[0], :] = piece
        pieces[i, piece.shape[0] :, :] = counts

    def scatter_copy(d):
        return pltpu.make_async_remote_copy(
            src_ref=pieces.at[lax.rem(f + d, n_fsdp)], dst_ref=plane_slots.at[f],
            send_sem=ps.at[d], recv_sem=pr.at[d], device_id=in_plane(d), device_id_type=mesh_id)

    def column_copy(d):
        return pltpu.make_async_remote_copy(
            src_ref=column_slots.at[g], dst_ref=column_slots.at[g],
            send_sem=cs.at[d], recv_sem=cr.at[d], device_id=in_column(d), device_id_type=mesh_id)

    def total_copy(d):
        return pltpu.make_async_remote_copy(
            src_ref=totals.at[f], dst_ref=totals.at[f],
            send_sem=ts.at[d], recv_sem=tr.at[d], device_id=in_plane(d), device_id_type=mesh_id)

    block = 4 * rank
    eye = jnp.where(
        lax.broadcasted_iota(jnp.int32, (block, block), 0) == lax.broadcasted_iota(jnp.int32, (block, block), 1),
        1.0, 0.0).astype(BF16)

    def turn(e):
        unit = lax.rem(my_unit + n_units - e, n_units)
        unit_rows = pl.ds(pl.multiple_of(unit * UNIT, UNIT), UNIT)
        for i in range(width // block):
            chunk = raw[unit_rows, i * block : (i + 1) * block]
            part = lax.dot_general(eye, chunk, NT, preferred_element_type=F32)
            for a in range(4):
                start = (4 * i + a) * pitch
                work[0, start : start + rank, :] = part[a * rank : (a + 1) * rank, :]
        for b in range(rank):
            turned[e, b * rank : (b + 1) * rank, :] = work[0, pl.ds(b, rank, stride=pitch), :].astype(BF16)

    def arrive(e):
        for kind, step, p in order:
            if step[0] == e:
                land(kind, step, p)

    pl.semaphore_wait(barrier, n_fsdp - 1 + n_grp - 1)
    for d in range(1, n_fsdp):
        scatter_copy(d).start()
    send_part(0)
    pass_copy(0).start()
    plane_slots[f] = pieces[f]
    flat = [
        jnp.concatenate([grad[a : a + 1, :] for a in range(rank)], axis=1) for grad in per_doc
    ]
    fresh = jnp.concatenate(
        flat + [jnp.zeros((spare - n_docs, width), F32)], axis=0).astype(BF16)
    score_rows[0, stored:, :] = fresh
    pass_copy(1).start()
    new_grads[...] = fresh[:n_docs]
    for d in range(1, n_fsdp):
        scatter_copy(d).wait()
    summed = plane_slots[0]
    for i in range(1, n_fsdp):
        summed = summed + plane_slots[i]
    column_slots[g] = summed
    for d in range(1, n_grp):
        column_copy(d).start()
    send_part(1)
    for d in range(1, n_grp):
        column_copy(d).wait()
    summed = column_slots[0]
    for i in range(1, n_grp):
        summed = summed + column_slots[i]
    totals[f] = summed
    for d in range(1, n_fsdp):
        total_copy(d).start()
    send_part(2)
    wide_row = lax.broadcasted_iota(jnp.int32, order_m.shape, 0)
    wide_lane = lax.broadcasted_iota(jnp.int32, order_m.shape, 1)
    from_core = lax.rem(wide_lane // here, 2)
    from_unit = lax.rem(my_unit + n_units - wide_lane // (2 * UNIT), n_units)
    from_row = (
        jnp.where(from_core == core, 0, mine) + from_unit * UNIT
        + lax.rem(wide_lane // (2 * here), UNIT // here) * here + lax.rem(wide_lane, here))
    order_m[...] = jnp.where(wide_row == from_row, 1.0, 0.0).astype(BF16)

    loads[4].wait()
    loads[5].wait()
    for d in range(1, n_fsdp):
        total_copy(d).wait()

    covariance = jnp.concatenate([totals[i, :share, :] for i in range(n_fsdp)], axis=0)
    covariance = covariance / summed[summed.shape[0] - 1 :, :]
    diagonal = (rows == lanes) | (rows + rank == lanes)
    on_diagonal = jnp.where(diagonal, covariance, 0.0)
    in_trace = jnp.sum(jnp.where(lanes < rank, on_diagonal, 0.0))
    out_trace = jnp.sum(jnp.where(lanes < rank, 0.0, on_diagonal))
    ridge = jnp.where(lanes < rank, 0.1 * in_trace / rank, 0.1 * out_trace / rank)
    both = invert_pair(covariance + jnp.where(diagonal, ridge, 0.0), rank)

    ih, im, il = split3(both[:, :rank])
    zero = jnp.zeros((rank, rank), BF16)
    in_left = jnp.concatenate([
        jnp.concatenate([ih, ih, ih], axis=1),
        jnp.concatenate([im, im, zero], axis=1),
        jnp.concatenate([il, zero, zero], axis=1)], axis=0)
    out_left = jnp.concatenate(split3(both[:, rank:]), axis=0)

    pass_copy(0).wait()
    pass_copy(1).wait()
    own_scores = []
    for e in range(n_units):
        arrive(e)
        turn(e)
        for b in range(0, rank, 2):
            right = jnp.concatenate([turned[e, (b + j) * rank : (b + j + 1) * rank, :] for j in range(2)], axis=1)
            part = jnp.dot(out_left, right, preferred_element_type=F32)
            part = part[:rank] + (part[rank : 2 * rank] + part[2 * rank :])
            for j in range(2):
                work[e, pl.ds(b + j, rank, stride=pitch), :] = part[:, j * UNIT : (j + 1) * UNIT]
        for a in range(0, rank, 2):
            half_done = jnp.concatenate(
                [work[e, (a + j) * pitch : (a + j) * pitch + rank, :] for j in range(2)], axis=1)
            right = jnp.concatenate(split3(half_done), axis=0)
            part = jnp.dot(in_left, right, preferred_element_type=F32)
            part = part[:rank] + (part[rank : 2 * rank] + part[2 * rank :])
            for j in range(2):
                own[e, (a + j) * rank : (a + j + 1) * rank, :] = part[:, j * UNIT : (j + 1) * UNIT].astype(BF16)
        if e < n_units - 1:
            both_rows = score_rows[...].reshape(2 * (stored + spare), width)
            both_scores = jnp.dot(both_rows, own[e], preferred_element_type=F32).astype(BF16)
            lent[e] = both_scores[stored + spare :]
            pass_copy(2 + e).start()
            own_scores.append(both_scores[: stored + spare])
        else:
            lent[e] = jnp.dot(score_rows[1], own[e], preferred_element_type=F32).astype(BF16)
            pass_copy(2 + e).start()
            own_scores.append(jnp.dot(score_rows[0], own[e], preferred_element_type=F32).astype(BF16))
    for e in range(n_units):
        pass_copy(2 + e).wait()
    scores = jnp.concatenate(own_scores + [borrowed[e] for e in range(n_units)], axis=1)
    scores = jnp.dot(scores, order_m[...], preferred_element_type=F32).astype(BF16)
    for kind, step, p in order:
        block_copy(kind, step, p).wait_send()
    store_out[...] = scores[:stored]
    new_out[...] = scores[stored : stored + n_docs]


PIECE = 16
UNIT = 128
AHEAD = 8
MARKS = (4, 6)


def hand_over(*refs):
    for source, target in zip(refs[:3], refs[3:]):
        target[...] = source[...]


def influence(n_grp, n_fsdp, doc_lengths, acts, out_grads, proj_in, proj_out, queries, store):
    n_docs = acts.shape[0]
    rank = proj_in.shape[0]
    here, width = queries.shape
    stored = store.shape[0]
    n_queries = n_fsdp * here
    dma = pltpu.SemaphoreType.DMA
    slot = (-(-(rank // n_fsdp) // 8) * 8 + 8, 2 * rank)
    score_rows = -(-(stored + n_docs) // 16) * 16
    copies = dma((n_fsdp // 2 * (here // PIECE),))
    mine = n_queries // 2
    results = pl.pallas_call(
        functools.partial(influence_kernel, n_grp, n_fsdp),
        out_shape=(
            VMEM((n_docs, width), BF16),
            VMEM((stored, n_queries), BF16),
            VMEM((n_docs, n_queries), BF16),
        ),
        in_specs=[pl.BlockSpec(memory_space=pltpu.SMEM)] + [pl.BlockSpec(memory_space=ANY)] * 6,
        out_specs=tuple([pl.BlockSpec(memory_space=VMEM)] * 3),
        scratch_shapes=[
            VMEM(acts.shape, BF16), VMEM(out_grads.shape, BF16),
            VMEM(proj_in.shape, BF16), VMEM(proj_out.shape, BF16),
            VMEM((mine, width), BF16), VMEM((mine // UNIT, width, UNIT), BF16),
            VMEM((mine // UNIT, width, UNIT), BF16), VMEM((2, score_rows, width), BF16),
            VMEM((mine // UNIT, rank * (rank + 8), UNIT), F32),
            VMEM((n_queries, n_queries), BF16),
            VMEM((mine // UNIT, score_rows, UNIT), BF16), VMEM((mine // UNIT, score_rows, UNIT), BF16),
            VMEM((n_fsdp,) + slot, F32), VMEM((n_fsdp,) + slot, F32),
            VMEM((n_grp,) + slot, F32), VMEM((n_fsdp,) + slot, F32),
            dma((6,)), copies, copies, dma((2 + mine // UNIT,)), dma((2 + mine // UNIT,)),
            dma((n_fsdp,)), dma((n_fsdp,)), dma((n_grp,)), dma((n_grp,)), dma((n_fsdp,)), dma((n_fsdp,)),
        ],
        compiler_params=pltpu.CompilerParams(
            collective_id=0, has_side_effects=True, vmem_limit_bytes=56 * 2**20),
    )(doc_lengths, acts, out_grads, proj_in, proj_out, queries, store)
    return pl.pallas_call(
        hand_over,
        out_shape=tuple(jax.ShapeDtypeStruct(r.shape, r.dtype) for r in results),
        in_specs=[pl.BlockSpec(memory_space=VMEM)] * 3,
        out_specs=tuple([pl.BlockSpec(memory_space=VMEM)] * 3),
        compiler_params=pltpu.CompilerParams(vmem_limit_bytes=4 * 2**20),
    )(*results)


def solution(mesh):
    n_grp, n_fsdp = mesh.shape["grp"], mesh.shape["fsdp"]

    def shards(acts, out_grads, doc_lengths, proj_in, proj_out, store_grads, queries):
        return influence(
            n_grp, n_fsdp, doc_lengths, acts, out_grads, proj_in, proj_out, queries, store_grads)

    rows = P(("grp", "fsdp"), None)
    placed = (
        P(("grp", "fsdp"), None, None),
        P(("grp", "fsdp"), None, None),
        P(("grp", "fsdp")),
        P(),
        P(),
        rows,
        P("fsdp", None),
    )
    return jax.shard_map(
        shards, mesh=mesh, in_specs=placed, out_specs=(rows, rows, rows), check_vma=False)
```
